32 devices in a mesh: gx: 4 (over x, core), gy: 8 (over z, y).
Axes of the slice: x: 2, y: 2, z: 4, core: 2. Of those that a mesh axis runs over, the one named last changes fastest.
Arguments:
- echoes: float32 [2, 256, 16384], P(None, ('gx', 'gy')), may hold values from -6 to 6
- range_ref: float32 [2, 1024], replicated, may hold values from -0.125 to 0.125
- azimuth_ref: float32 [2, 512], replicated, may hold values from -0.1875 to 0.1875
- shift_bins: int32 [256], P(('gx', 'gy')), may hold values from -28 to 28, as said below
- interp_weights: float32 [256, 8], P(('gx', 'gy')), may hold values from -2.5 to 2.5
Outputs:
- image: float32 [2, 256, 16384], P(None, None, ('gx', 'gy'))
The draws below stay inside these ranges and needn't reach their ends.
Inputs may be any that keep to these rules, and one draw needn't show every extreme that they name: `shift_bins`: both -28 and 28 occur among the offsets.
All inputs are finite; a program needn't handle non-finite values.
Results may differ from the reference program's by a relative error of at most 0.00007.
Values sent between devices are 32-bit elements; how exact they have to be, the bound alone decides.
No kernel may reach another device: no remote copies, remote signals or barrier semaphores. Data moves between devices by JAX's collectives and lax.ppermute only.
A program may use at most 64 MiB of HBM per device.

```python
import jax
import jax.numpy as jnp
from jax import lax

NR = 16384
KR = 1024
KA = 512
TAPS = 8
MAXOFF = 28
NA = 256
HALO = 32


def draw_shift_bins(key, part):
    key_base = jax.random.fold_in(key, 11)
    key_first = jax.random.fold_in(key, 12)
    key_step = jax.random.fold_in(key, 13)
    base = jax.random.randint(key_base, (NA,), 0 - MAXOFF, MAXOFF + 1)
    first = jax.random.randint(key_first, (), 0, NA)
    step = jax.random.randint(key_step, (), 1, NA)
    second = (first + step) % NA
    base = base.at[first].set(MAXOFF)
    base = base.at[second].set(0 - MAXOFF)
    return base.astype(jnp.int32)


def levels(rng, shape, cuts, least, largest):
    factor_of, own = 1.0, jax.random.fold_in(rng, 6)
    for axis_at, shards_of in cuts:
        draws = jnp.exp(jax.random.uniform(jax.random.fold_in(own, axis_at), (shards_of,), jnp.float32, least / len(cuts), largest / len(cuts)))
        factor_of = factor_of * jnp.repeat(draws, shape[axis_at] // shards_of).reshape([-1 if axis == axis_at else 1 for axis in range(len(shape))])
    return factor_of


def centred(own_key, extent, scale, bound, shards=(), kind=jnp.bfloat16):
    values = scale * jax.random.normal(own_key, extent, jnp.float32)
    if shards:
        values = values * levels(own_key, extent, shards, -0.22, 0.18)
    return jnp.clip(values, -bound, bound).astype(kind)


def setup_inputs(seed: int = 0) -> dict:
    streams_of = jax.random.split(jax.random.key(seed), 6)
    echoes = centred(streams_of[0], (2, NA, NR), 1.0, 6.0, ((1, 32),), jnp.float32)
    range_ref = centred(streams_of[1], (2, KR), (2 * KR) ** -0.5, 0.125, (), jnp.float32)
    azimuth_ref = centred(streams_of[2], (2, KA), (2 * KA) ** -0.5, 0.1875, (), jnp.float32)
    shift_bins = draw_shift_bins(jax.random.fold_in(streams_of[5], 71), 0)
    interp_weights = centred(streams_of[4], (NA, TAPS), 0.35, 2.5, ((0, 32),), jnp.float32)
    return {"echoes": echoes, "range_ref": range_ref, "azimuth_ref": azimuth_ref, "shift_bins": shift_bins, "interp_weights": interp_weights}


def compress_range(lines, range_ref):
    signal = lax.complex(lines[0], lines[1])
    kernel = lax.complex(range_ref[0], range_ref[1])
    length = NR + KR
    spectrum = jnp.fft.fft(signal, n=length, axis=1) * jnp.conj(jnp.fft.fft(kernel, n=length))[None, :]
    product = jnp.roll(jnp.fft.ifft(spectrum, axis=1), KR // 2, axis=1)[:, :NR]
    return jnp.stack([jnp.real(product), jnp.imag(product)])


def compress_azimuth(columns, azimuth_ref):
    signal = lax.complex(columns[0], columns[1])
    kernel = lax.complex(azimuth_ref[0], azimuth_ref[1])
    length = NA + KA
    spectrum = jnp.fft.fft(signal, n=length, axis=0) * jnp.conj(jnp.fft.fft(kernel, n=length))[:, None]
    product = jnp.roll(jnp.fft.ifft(spectrum, axis=0), KA // 2, axis=0)[:NA]
    return jnp.stack([jnp.real(product), jnp.imag(product)])


def migrate(compressed, offsets, weights):
    extended = jnp.pad(compressed, ((0, 0), (0, 0), (HALO, HALO)))
    span = NR + TAPS - 1
    positions = HALO + offsets[:, None] - (TAPS // 2 - 1) + jnp.arange(span, dtype=jnp.int32)[None, :]
    positions = jnp.broadcast_to(positions[None], (2,) + positions.shape)
    shifted = jnp.take_along_axis(extended, positions, axis=2)
    total = weights[None, :, 0, None] * shifted[:, :, 0:NR]
    for column in range(1, TAPS):
        total = total + weights[None, :, column, None] * shifted[:, :, column:column + NR]
    return total


def reference(echoes, range_ref, azimuth_ref, shift_bins, interp_weights):
    block = KA // 2
    count = NA // block
    grouped = echoes.reshape(2, count, block, NR).transpose(1, 0, 2, 3)
    offsets = shift_bins.reshape(count, block)
    weights = interp_weights.reshape(count, block, TAPS)

    def line_section(items):
        lines, offs, wts = items
        return migrate(compress_range(lines, range_ref), offs, wts)

    migrated = lax.map(line_section, (grouped, offsets, weights))
    migrated = migrated.transpose(1, 0, 2, 3).reshape(2, NA, NR)
    width = KR // 2
    pieces = NR // width
    columns = migrated.reshape(2, NA, pieces, width).transpose(2, 0, 1, 3)
    focused = lax.map(lambda column_block: compress_azimuth(column_block, azimuth_ref), columns)
    return focused.transpose(1, 2, 0, 3).reshape(2, NA, NR)
```

```python
import functools

import jax
import jax.numpy as jnp
from jax import lax
from jax.experimental import pallas as pl
from jax.experimental.pallas import tpu as pltpu
from jax.sharding import PartitionSpec as P

TAPS = 8
BLOCK = 256
LANE = 128
AXES = ("gx", "gy")
ROWS_BY_ROWS = (((1,), (1,)), ((), ()))
PLAIN = (((1,), (0,)), ((), ()))


def split(values):
    high = values.astype(jnp.bfloat16)
    return high, (values - high.astype(jnp.float32)).astype(jnp.bfloat16)


def toeplitz(row, rows, width):
    row = jnp.concatenate([row, jnp.zeros((1, width - row.shape[1]), jnp.float32)], axis=1)
    return pltpu.roll(jnp.broadcast_to(row, (rows, width)), 0, axis=1, stride=1, stride_axis=0)


def range_kernel(
    component, lines, count, sections,
    shift_hbm, taps_hbm, weights_hbm, echoes_hbm, out_ref,
    shift_ref, taps_ref, weights_ref, echoes_ref, even, odd, table, compressed, sems,
):
    pairs = (
        (taps_hbm, taps_ref), (echoes_hbm, echoes_ref), (shift_hbm, shift_ref), (weights_hbm, weights_ref),
    )
    copies = [pltpu.make_async_copy(src, dst, sems.at[n]) for n, (src, dst) in enumerate(pairs)]
    for copy in copies:
        copy.start()
    half = (sections - 1) // 2
    rows = count * lines
    total = count + 2 * half
    copies[0].wait()
    for part in range(2):
        row = taps_ref[part : part + 1, :]
        if component == 1 and part == 1:
            row = 0.0 - row
        table[part, 0], table[part, 1] = split(toeplitz(row, BLOCK, sections * BLOCK))
    copies[1].wait()
    for part in range(2):
        source = part if component == 0 else 1 - part

        def piece(block):
            at = block - half
            if 0 <= at < count:
                return echoes_ref[source, :, at * BLOCK : (at + 1) * BLOCK]
            return jnp.zeros((lines, BLOCK), jnp.float32)

        for offset, ref in ((0, even), (1, odd)):
            for pair in range((total - offset) // 2):
                first = 2 * pair + offset
                both = jnp.concatenate([piece(first), piece(first + 1)], axis=0)
                at = slice(pair * 2 * lines, (pair + 1) * 2 * lines)
                ref[part, 0, at, :], ref[part, 1, at, :] = split(both)
    sums = None
    for part in range(2):
        for section in range(sections):
            ref = even if section % 2 == 0 else odd
            start = (section - section % 2) * lines
            x_high = ref[part, 0, start : start + rows, :]
            x_low = ref[part, 1, start : start + rows, :]
            at = slice(section * BLOCK, (section + 1) * BLOCK)
            t_high, t_low = table[part, 0, :, at], table[part, 1, :, at]
            for left, right in ((x_high, t_high), (x_low, t_high), (x_high, t_low)):
                term = lax.dot_general(left, right, ROWS_BY_ROWS, preferred_element_type=jnp.float32)
                sums = term if sums is None else sums + term
    compressed[0:lines, :] = jnp.zeros((lines, BLOCK), jnp.float32)
    compressed[lines : lines + rows, :] = sums
    compressed[lines + rows :, :] = jnp.zeros((lines, BLOCK), jnp.float32)
    copies[2].wait()
    copies[3].wait()
    migrate(lines, 2 * count, shift_ref, weights_ref, compressed, out_ref)


def migrate(lines, tiles, shift_ref, weights_ref, compressed, out_ref):
    per = out_ref.shape[2] // LANE
    lane = lax.broadcasted_iota(jnp.int32, (lines, LANE), 1)
    row = lax.broadcasted_iota(jnp.int32, (lines, LANE), 0)
    shift = jnp.zeros((lines, LANE), jnp.int32)
    for line in range(lines):
        shift = jnp.where(row == line, shift_ref[line], shift)
    places = [lane + shift - (TAPS // 2 - 1) + step for step in range(2)]
    index = [place & (LANE - 1) for place in places]
    before = [place < 0 for place in places]
    after = [place >= LANE for place in places]
    weight = [jnp.broadcast_to(weights_ref[:, j : j + 1], (lines, LANE)) for j in range(TAPS)]
    inside = lane < LANE - 2

    def turned(tile, step):
        block = tile // 2 + 1
        at = (tile % 2) * LANE
        values = compressed[block * lines : (block + 1) * lines, at : at + LANE]
        return jnp.take_along_axis(values, index[step], axis=1, mode="promise_in_bounds")

    later = [turned(tiles + 1, step) for step in range(2)]
    here = [turned(tiles, step) for step in range(2)]
    carried = [jnp.zeros((lines, LANE), jnp.float32)] * 3
    for tile in range(tiles, -1, -1):
        earlier = [turned(tile - 1, step) for step in range(2)]
        pair = [
            jnp.where(before[step], earlier[step], jnp.where(after[step], later[step], here[step]))
            for step in range(2)
        ]
        total = None
        for k in (3, 2, 1, 0):
            term = weight[2 * k] * pair[0] + weight[2 * k + 1] * pair[1]
            if total is None:
                total = term
            else:
                rolled = pltpu.roll(total, LANE - 2, axis=1)
                total = jnp.where(inside, rolled, carried[k]) + term
                carried[k] = rolled
        if tile < tiles:
            at = (tile % per) * LANE
            out_ref[tile // per, :, at : at + LANE] = total
        later, here = here, earlier


def range_call(component, echoes, range_ref, shift_bins, weights, devices_all):
    lines, range_total = echoes.shape[1], echoes.shape[2]
    count = range_total // BLOCK
    sections = range_ref.shape[1] // BLOCK + 1
    padded = (count + sections - 1) * lines
    bins = range_total // devices_all
    flops = 2 * 3 * 2 * count * lines * sections * BLOCK * BLOCK
    return pl.pallas_call(
        functools.partial(range_kernel, component, lines, count, sections),
        out_shape=jax.ShapeDtypeStruct((devices_all, lines, bins), jnp.float32),
        in_specs=[pl.BlockSpec(memory_space=pl.ANY)] * 4,
        out_specs=pl.BlockSpec(memory_space=pltpu.VMEM),
        scratch_shapes=[
            pltpu.SMEM(shift_bins.shape, jnp.int32),
            pltpu.VMEM(range_ref.shape, jnp.float32),
            pltpu.VMEM(weights.shape, jnp.float32),
            pltpu.VMEM(echoes.shape, jnp.float32),
            pltpu.VMEM((2, 2, padded, BLOCK), jnp.bfloat16),
            pltpu.VMEM((2, 2, padded, BLOCK), jnp.bfloat16),
            pltpu.VMEM((2, 2, BLOCK, sections * BLOCK), jnp.bfloat16),
            pltpu.VMEM(((count + 2) * lines, BLOCK), jnp.float32),
            pltpu.SemaphoreType.DMA((4,)),
        ],
        compiler_params=pltpu.CompilerParams(vmem_limit_bytes=40 << 20),
        cost_estimate=pl.CostEstimate(flops=flops, bytes_accessed=3 * echoes.size * 2, transcendentals=0),
        name="range_" + str(component),
    )(shift_bins, range_ref, weights, echoes)


def azimuth_tables(taps_ref, table):
    length = taps_ref.shape[1]
    diagonals = table.shape[2]
    for part in range(2):
        row = jnp.concatenate(
            [jnp.zeros((1, BLOCK), jnp.float32), taps_ref[part : part + 1, :]], axis=1
        )
        full = toeplitz(row, BLOCK, length + 2 * BLOCK)
        for diagonal in range(diagonals):
            at = (diagonal + 1) * BLOCK
            table[part, 0, diagonal], table[part, 1, diagonal] = split(full[:, at : at + BLOCK])


def azimuth_kernel(component, *refs):
    if component == 0:
        taps_ref, lines_ref, out_ref, table = refs
    else:
        taps_ref, lines_ref, earlier_ref, out_ref, table = refs
    azimuth_tables(taps_ref, table)
    diagonals = table.shape[2]
    middle = diagonals // 2
    blocks = lines_ref.shape[0] // BLOCK
    pieces = [split(lines_ref[b * BLOCK : (b + 1) * BLOCK, :]) for b in range(blocks)]
    for b in range(blocks):
        at = slice(b * BLOCK, (b + 1) * BLOCK)
        for part in range(2):
            sums = None
            for diagonal in range(diagonals):
                other = b + diagonal - middle
                if not 0 <= other < blocks:
                    continue
                m_high, m_low = pieces[other]
                t_high, t_low = table[part, 0, diagonal], table[part, 1, diagonal]
                for left, right in ((t_high, m_high), (t_high, m_low), (t_low, m_high)):
                    term = lax.dot_general(left, right, PLAIN, preferred_element_type=jnp.float32)
                    sums = term if sums is None else sums + term
            if component == 0:
                out_ref[part, at, :] = sums if part == 0 else 0.0 - sums
            else:
                out_ref[1 - part, at, :] = earlier_ref[1 - part, at, :] + sums


def azimuth_call(component, azimuth_ref, lines, earlier=None):
    count, bins = lines.shape
    diagonals = azimuth_ref.shape[1] // BLOCK + 1
    operands = [azimuth_ref, lines] + ([] if earlier is None else [earlier])
    return pl.pallas_call(
        functools.partial(azimuth_kernel, component),
        out_shape=jax.ShapeDtypeStruct((2, count, bins), jnp.float32),
        in_specs=[pl.BlockSpec(memory_space=pltpu.VMEM)] * len(operands),
        out_specs=pl.BlockSpec(memory_space=pltpu.VMEM),
        scratch_shapes=[pltpu.VMEM((2, 2, diagonals, BLOCK, BLOCK), jnp.bfloat16)],
        compiler_params=pltpu.CompilerParams(vmem_limit_bytes=40 << 20),
        cost_estimate=pl.CostEstimate(
            flops=2 * 3 * 2 * count * BLOCK * bins, bytes_accessed=4 * 3 * count * bins, transcendentals=0
        ),
        name="azimuth_" + str(component),
    )(*operands)


def per_device(echoes, range_ref, azimuth_ref, shift_bins, interp_weights):
    devices_all = lax.axis_size(AXES)
    lines_total = devices_all * echoes.shape[1]
    image = None
    for component in range(2):
        migrated = range_call(component, echoes, range_ref, shift_bins, interp_weights, devices_all)
        moved = lax.all_to_all(migrated, AXES, split_axis=0, concat_axis=0, tiled=True)
        image = azimuth_call(component, azimuth_ref, moved.reshape(lines_total, -1), image)
    return image


def solution(mesh):
    placed = (P(None, AXES, None), P(), P(), P(AXES), P(AXES, None))
    return jax.shard_map(
        per_device,
        mesh=mesh,
        in_specs=placed,
        out_specs=P(None, None, AXES),
        check_vma=False,
    )
```

```python
import functools

import jax
import jax.numpy as jnp
from jax import lax
from jax.experimental import pallas as pl
from jax.experimental.pallas import tpu as pltpu
from jax.sharding import PartitionSpec as P

TAPS = 8
BLOCK = 256
LANE = 128
AXES = ("gx", "gy")
ROWS_BY_ROWS = (((1,), (1,)), ((), ()))
PLAIN = (((1,), (0,)), ((), ()))


def split(values):
    high = values.astype(jnp.bfloat16)
    return high, (values - high.astype(jnp.float32)).astype(jnp.bfloat16)


def toeplitz(row, rows, width):
    row = jnp.concatenate([row, jnp.zeros((1, width - row.shape[1]), jnp.float32)], axis=1)
    return pltpu.roll(jnp.broadcast_to(row, (rows, width)), 0, axis=1, stride=1, stride_axis=0)


def range_kernel(
    component, lines, count, sections,
    shift_ref, taps_hbm, weights_hbm, echoes_hbm, out_ref,
    taps_ref, weights_ref, echoes_ref, even, odd, table, compressed, sems,
):
    pairs = ((taps_hbm, taps_ref), (echoes_hbm, echoes_ref), (weights_hbm, weights_ref))
    copies = [pltpu.make_async_copy(src, dst, sems.at[n]) for n, (src, dst) in enumerate(pairs)]
    for copy in copies:
        copy.start()
    half = (sections - 1) // 2
    rows = count * lines
    total = count + 2 * half
    copies[0].wait()
    copies[2].wait()
    for part in range(2):
        row = taps_ref[part : part + 1, :]
        if component == 1 and part == 1:
            row = 0.0 - row
        table[part, 0], table[part, 1] = split(toeplitz(row, BLOCK, sections * BLOCK))
    copies[1].wait()
    for part in range(2):
        source = part if component == 0 else 1 - part

        def piece(block):
            at = block - half
            if 0 <= at < count:
                return echoes_ref[source, :, at * BLOCK : (at + 1) * BLOCK]
            return jnp.zeros((lines, BLOCK), jnp.float32)

        for offset, ref in ((0, even), (1, odd)):
            for pair in range((total - offset) // 2):
                first = 2 * pair + offset
                both = jnp.concatenate([piece(first), piece(first + 1)], axis=0)
                at = slice(pair * 2 * lines, (pair + 1) * 2 * lines)
                ref[part, 0, at, :], ref[part, 1, at, :] = split(both)
    sums = None
    for part in range(2):
        for section in range(sections):
            ref = even if section % 2 == 0 else odd
            start = (section - section % 2) * lines
            x_high = ref[part, 0, start : start + rows, :]
            x_low = ref[part, 1, start : start + rows, :]
            at = slice(section * BLOCK, (section + 1) * BLOCK)
            t_high, t_low = table[part, 0, :, at], table[part, 1, :, at]
            for left, right in ((x_high, t_high), (x_low, t_high), (x_high, t_low)):
                term = lax.dot_general(left, right, ROWS_BY_ROWS, preferred_element_type=jnp.float32)
                sums = term if sums is None else sums + term
    compressed[0:lines, :] = jnp.zeros((lines, BLOCK), jnp.float32)
    compressed[lines : lines + rows, :] = sums
    compressed[lines + rows :, :] = jnp.zeros((lines, BLOCK), jnp.float32)
    migrate(lines, 2 * count, shift_ref, weights_ref, compressed, out_ref)


def migrate(lines, tiles, shift_ref, weights_ref, compressed, out_ref):
    per = out_ref.shape[2] // LANE
    lane = lax.broadcasted_iota(jnp.int32, (lines, LANE), 1)
    row = lax.broadcasted_iota(jnp.int32, (lines, LANE), 0)
    shift = jnp.zeros((lines, LANE), jnp.int32)
    for line in range(lines):
        shift = jnp.where(row == line, shift_ref[line], shift)
    places = [lane + shift - (TAPS // 2 - 1) + step for step in range(2)]
    index = [place & (LANE - 1) for place in places]
    before = [place < 0 for place in places]
    after = [place >= LANE for place in places]
    weight = [jnp.broadcast_to(weights_ref[:, j : j + 1], (lines, LANE)) for j in range(TAPS)]
    inside = lane < LANE - 2

    def turned(tile, step):
        block = tile // 2 + 1
        at = (tile % 2) * LANE
        values = compressed[block * lines : (block + 1) * lines, at : at + LANE]
        return jnp.take_along_axis(values, index[step], axis=1, mode="promise_in_bounds")

    later = [turned(tiles + 1, step) for step in range(2)]
    here = [turned(tiles, step) for step in range(2)]
    carried = [jnp.zeros((lines, LANE), jnp.float32)] * 3
    for tile in range(tiles, -1, -1):
        earlier = [turned(tile - 1, step) for step in range(2)]
        pair = [
            jnp.where(before[step], earlier[step], jnp.where(after[step], later[step], here[step]))
            for step in range(2)
        ]
        total = None
        for k in (3, 2, 1, 0):
            term = weight[2 * k] * pair[0] + weight[2 * k + 1] * pair[1]
            if total is None:
                total = term
            else:
                rolled = pltpu.roll(total, LANE - 2, axis=1)
                total = jnp.where(inside, rolled, carried[k]) + term
                carried[k] = rolled
        if tile < tiles:
            at = (tile % per) * LANE
            out_ref[tile // per, :, at : at + LANE] = total
        later, here = here, earlier


def range_call(component, echoes, range_ref, shift_bins, weights, devices_all):
    lines, range_total = echoes.shape[1], echoes.shape[2]
    count = range_total // BLOCK
    sections = range_ref.shape[1] // BLOCK + 1
    padded = (count + sections - 1) * lines
    bins = range_total // devices_all
    flops = 2 * 3 * 2 * count * lines * sections * BLOCK * BLOCK
    return pl.pallas_call(
        functools.partial(range_kernel, component, lines, count, sections),
        out_shape=jax.ShapeDtypeStruct((devices_all, lines, bins), jnp.float32),
        in_specs=[pl.BlockSpec(memory_space=pltpu.SMEM)] + [pl.BlockSpec(memory_space=pltpu.HBM)] * 3,
        out_specs=pl.BlockSpec(memory_space=pltpu.VMEM),
        scratch_shapes=[
            pltpu.VMEM(range_ref.shape, jnp.float32),
            pltpu.VMEM(weights.shape, jnp.float32),
            pltpu.VMEM(echoes.shape, jnp.float32),
            pltpu.VMEM((2, 2, padded, BLOCK), jnp.bfloat16),
            pltpu.VMEM((2, 2, padded, BLOCK), jnp.bfloat16),
            pltpu.VMEM((2, 2, BLOCK, sections * BLOCK), jnp.bfloat16),
            pltpu.VMEM(((count + 2) * lines, BLOCK), jnp.float32),
            pltpu.SemaphoreType.DMA((3,)),
        ],
        compiler_params=pltpu.CompilerParams(vmem_limit_bytes=60 << 20),
        cost_estimate=pl.CostEstimate(flops=flops, bytes_accessed=3 * echoes.size * 2, transcendentals=0),
        name="range_" + str(component),
    )(shift_bins, range_ref, weights, echoes)


def azimuth_tables(taps_ref, table):
    length = taps_ref.shape[1]
    diagonals = table.shape[2]
    for part in range(2):
        row = jnp.concatenate(
            [jnp.zeros((1, BLOCK), jnp.float32), taps_ref[part : part + 1, :]], axis=1
        )
        full = toeplitz(row, BLOCK, length + 2 * BLOCK)
        for diagonal in range(diagonals):
            at = (diagonal + 1) * BLOCK
            table[part, 0, diagonal], table[part, 1, diagonal] = split(full[:, at : at + BLOCK])


def azimuth_kernel(component, *refs):
    if component == 0:
        taps_ref, lines_ref, out_ref, table = refs
    else:
        taps_ref, lines_ref, earlier_ref, out_ref, table = refs
    azimuth_tables(taps_ref, table)
    diagonals = table.shape[2]
    middle = diagonals // 2
    blocks = lines_ref.shape[0] // BLOCK
    pieces = [split(lines_ref[b * BLOCK : (b + 1) * BLOCK, :]) for b in range(blocks)]
    for b in range(blocks):
        at = slice(b * BLOCK, (b + 1) * BLOCK)
        for part in range(2):
            sums = None
            for diagonal in range(diagonals):
                other = b + diagonal - middle
                if not 0 <= other < blocks:
                    continue
                m_high, m_low = pieces[other]
                t_high, t_low = table[part, 0, diagonal], table[part, 1, diagonal]
                for left, right in ((t_high, m_high), (t_high, m_low), (t_low, m_high)):
                    term = lax.dot_general(left, right, PLAIN, preferred_element_type=jnp.float32)
                    sums = term if sums is None else sums + term
            if component == 0:
                out_ref[part, at, :] = sums if part == 0 else 0.0 - sums
            else:
                out_ref[1 - part, at, :] = earlier_ref[1 - part, at, :] + sums


def azimuth_call(component, azimuth_ref, lines, earlier=None):
    count, bins = lines.shape
    diagonals = azimuth_ref.shape[1] // BLOCK + 1
    operands = [azimuth_ref, lines] + ([] if earlier is None else [earlier])
    return pl.pallas_call(
        functools.partial(azimuth_kernel, component),
        out_shape=jax.ShapeDtypeStruct((2, count, bins), jnp.float32),
        in_specs=[pl.BlockSpec(memory_space=pltpu.VMEM)] * len(operands),
        out_specs=pl.BlockSpec(memory_space=pltpu.VMEM),
        scratch_shapes=[pltpu.VMEM((2, 2, diagonals, BLOCK, BLOCK), jnp.bfloat16)],
        compiler_params=pltpu.CompilerParams(vmem_limit_bytes=40 << 20),
        cost_estimate=pl.CostEstimate(
            flops=2 * 3 * 2 * count * BLOCK * bins, bytes_accessed=4 * 3 * count * bins, transcendentals=0
        ),
        name="azimuth_" + str(component),
    )(*operands)


def per_device(echoes, range_ref, azimuth_ref, shift_bins, interp_weights):
    devices_all = lax.axis_size(AXES)
    lines_total = devices_all * echoes.shape[1]
    image = None
    for component in range(2):
        migrated = range_call(component, echoes, range_ref, shift_bins, interp_weights, devices_all)
        moved = lax.all_to_all(migrated, AXES, split_axis=0, concat_axis=0, tiled=True)
        image = azimuth_call(component, azimuth_ref, moved.reshape(lines_total, -1), image)
    return image


def solution(mesh):
    placed = (P(None, AXES, None), P(), P(), P(AXES), P(AXES, None))
    return jax.shard_map(
        per_device,
        mesh=mesh,
        in_specs=placed,
        out_specs=P(None, None, AXES),
        check_vma=False,
    )
```

```python
import functools

import jax
import jax.numpy as jnp
from jax import lax
from jax.experimental import pallas as pl
from jax.experimental.pallas import tpu as pltpu
from jax.sharding import PartitionSpec as P

TAPS = 8
BLOCK = 256
LANE = 128
AXES = ("gx", "gy")
LEVELS = 4
ROWS_BY_ROWS = (((1,), (1,)), ((), ()))
PLAIN = (((1,), (0,)), ((), ()))


def split(values):
    high = values.astype(jnp.bfloat16)
    return high, (values - high.astype(jnp.float32)).astype(jnp.bfloat16)


def toeplitz(row, rows, width):
    row = jnp.concatenate([row, jnp.zeros((1, width - row.shape[1]), jnp.float32)], axis=1)
    return pltpu.roll(jnp.broadcast_to(row, (rows, width)), 0, axis=1, stride=1, stride_axis=0)


def range_kernel(component, lines, count, sections, shift_ref, taps_hbm, weights_hbm, echoes_hbm, *refs):
    if component == 0:
        *outs, taps_ref, weights_ref, echoes_ref, even, odd, table, compressed, sems, ready, out_sems = refs
    else:
        ready, taps_ref, weights_ref, echoes_ref, even, odd, table, compressed, sems = refs
    pairs = ((taps_hbm, taps_ref), (echoes_hbm, echoes_ref), (weights_hbm, weights_ref))
    copies = [pltpu.make_async_copy(src, dst, sems.at[n]) for n, (src, dst) in enumerate(pairs)]
    for copy in copies:
        copy.start()
    half = (sections - 1) // 2
    rows = count * lines
    total = count + 2 * half
    copies[0].wait()
    copies[2].wait()
    for part in range(2):
        row = taps_ref[part : part + 1, :]
        if component == 1 and part == 1:
            row = 0.0 - row
        table[part, 0], table[part, 1] = split(toeplitz(row, BLOCK, sections * BLOCK))
    copies[1].wait()
    for part in range(2):
        source = part if component == 0 else 1 - part

        def piece(block):
            at = block - half
            if 0 <= at < count:
                return echoes_ref[source, :, at * BLOCK : (at + 1) * BLOCK]
            return jnp.zeros((lines, BLOCK), jnp.float32)

        for offset, ref in ((0, even), (1, odd)):
            for pair in range((total - offset) // 2):
                first = 2 * pair + offset
                both = jnp.concatenate([piece(first), piece(first + 1)], axis=0)
                at = slice(pair * 2 * lines, (pair + 1) * 2 * lines)
                ref[part, 0, at, :], ref[part, 1, at, :] = split(both)
    sums = None
    for part in range(2):
        for section in range(sections):
            ref = even if section % 2 == 0 else odd
            start = (section - section % 2) * lines
            x_high = ref[part, 0, start : start + rows, :]
            x_low = ref[part, 1, start : start + rows, :]
            at = slice(section * BLOCK, (section + 1) * BLOCK)
            t_high, t_low = table[part, 0, :, at], table[part, 1, :, at]
            for left, right in ((x_high, t_high), (x_low, t_high), (x_high, t_low)):
                term = lax.dot_general(left, right, ROWS_BY_ROWS, preferred_element_type=jnp.float32)
                sums = term if sums is None else sums + term
    compressed[0:lines, :] = jnp.zeros((lines, BLOCK), jnp.float32)
    compressed[lines : lines + rows, :] = sums
    compressed[lines + rows :, :] = jnp.zeros((lines, BLOCK), jnp.float32)
    migrate(lines, 2 * count, shift_ref, weights_ref, compressed, ready)
    if component == 0:
        mine = lax.axis_index("gy") // (ready.shape[2])
        sends = []
        for k, out in enumerate(outs):
            sends.append(pltpu.make_async_copy(ready.at[:, mine ^ k], out, out_sems.at[k]))
            sends[-1].start()
        for send in sends:
            send.wait()


def place_of(device, shape):
    at = []
    for extent in reversed(shape[:-2]):
        at.insert(0, device % extent)
        device //= extent
    return at


def migrate(lines, tiles, shift_ref, weights_ref, compressed, out_ref):
    per = out_ref.shape[-1] // LANE
    lane = lax.broadcasted_iota(jnp.int32, (lines, LANE), 1)
    row = lax.broadcasted_iota(jnp.int32, (lines, LANE), 0)
    shift = jnp.zeros((lines, LANE), jnp.int32)
    for line in range(lines):
        shift = jnp.where(row == line, shift_ref[line], shift)
    places = [lane + shift - (TAPS // 2 - 1) + step for step in range(2)]
    index = [place & (LANE - 1) for place in places]
    before = [place < 0 for place in places]
    after = [place >= LANE for place in places]
    weight = [jnp.broadcast_to(weights_ref[:, j : j + 1], (lines, LANE)) for j in range(TAPS)]
    inside = lane < LANE - 2

    def turned(tile, step):
        block = tile // 2 + 1
        at = (tile % 2) * LANE
        values = compressed[block * lines : (block + 1) * lines, at : at + LANE]
        return jnp.take_along_axis(values, index[step], axis=1, mode="promise_in_bounds")

    later = [turned(tiles + 1, step) for step in range(2)]
    here = [turned(tiles, step) for step in range(2)]
    carried = [jnp.zeros((lines, LANE), jnp.float32)] * 3
    for tile in range(tiles, -1, -1):
        earlier = [turned(tile - 1, step) for step in range(2)]
        pair = [
            jnp.where(before[step], earlier[step], jnp.where(after[step], later[step], here[step]))
            for step in range(2)
        ]
        total = None
        for k in (3, 2, 1, 0):
            term = weight[2 * k] * pair[0] + weight[2 * k + 1] * pair[1]
            if total is None:
                total = term
            else:
                rolled = pltpu.roll(total, LANE - 2, axis=1)
                total = jnp.where(inside, rolled, carried[k]) + term
                carried[k] = rolled
        if tile < tiles:
            at = (tile % per) * LANE
            out_ref[(*place_of(tile // per, out_ref.shape), slice(None), slice(at, at + LANE))] = total
        later, here = here, earlier


def range_call(component, echoes, range_ref, shift_bins, weights, planes):
    lines, range_total = echoes.shape[1], echoes.shape[2]
    count = range_total // BLOCK
    sections = range_ref.shape[1] // BLOCK + 1
    padded = (count + sections - 1) * lines
    outer, levels, inner = planes
    bins = range_total // (outer * levels * inner)
    flops = 2 * 3 * 2 * count * lines * sections * BLOCK * BLOCK
    scratch = [
        pltpu.VMEM(range_ref.shape, jnp.float32),
        pltpu.VMEM(weights.shape, jnp.float32),
        pltpu.VMEM(echoes.shape, jnp.float32),
        pltpu.VMEM((2, 2, padded, BLOCK), jnp.bfloat16),
        pltpu.VMEM((2, 2, padded, BLOCK), jnp.bfloat16),
        pltpu.VMEM((2, 2, BLOCK, sections * BLOCK), jnp.bfloat16),
        pltpu.VMEM(((count + 2) * lines, BLOCK), jnp.float32),
        pltpu.SemaphoreType.DMA((3,)),
    ]
    if component == 0:
        out_shape = [jax.ShapeDtypeStruct((outer, inner, lines, bins), jnp.float32)] * levels
        out_specs = [pl.BlockSpec(memory_space=pltpu.HBM)] * levels
        scratch += [
            pltpu.VMEM((outer, levels, inner, lines, bins), jnp.float32),
            pltpu.SemaphoreType.DMA((levels,)),
        ]
    else:
        out_shape = jax.ShapeDtypeStruct((outer * levels * inner, lines, bins), jnp.float32)
        out_specs = pl.BlockSpec(memory_space=pltpu.VMEM)
    return pl.pallas_call(
        functools.partial(range_kernel, component, lines, count, sections),
        out_shape=out_shape,
        in_specs=[pl.BlockSpec(memory_space=pltpu.SMEM)] + [pl.BlockSpec(memory_space=pltpu.HBM)] * 3,
        out_specs=out_specs,
        scratch_shapes=scratch,
        compiler_params=pltpu.CompilerParams(vmem_limit_bytes=60 << 20),
        cost_estimate=pl.CostEstimate(flops=flops, bytes_accessed=3 * echoes.size * 2, transcendentals=0),
        name="range_" + str(component),
    )(shift_bins, range_ref, weights, echoes)


def regroup_kernel(levels, plane, *refs):
    sources, outs, sems = refs[:levels], refs[levels:-1], refs[-1]
    inner = sources[0].shape[1]
    mine = lax.axis_index("gx") * inner + lax.rem(lax.axis_index("gy"), inner)
    copies = []
    for q in range(plane):
        place = mine ^ q
        for k in range(levels):
            source = sources[k].at[place // inner, lax.rem(place, inner)]
            copies.append(pltpu.make_async_copy(source, outs[q].at[k], sems.at[q, k]))
            copies[-1].start()
    for copy in copies:
        copy.wait()


def regroup_call(received):
    levels = len(received)
    outer, inner, lines, bins = received[0].shape
    plane = outer * inner
    return pl.pallas_call(
        functools.partial(regroup_kernel, levels, plane),
        out_shape=[jax.ShapeDtypeStruct((levels, lines, bins), jnp.float32)] * plane,
        in_specs=[pl.BlockSpec(memory_space=pl.ANY)] * levels,
        out_specs=[pl.BlockSpec(memory_space=pltpu.HBM)] * plane,
        scratch_shapes=[pltpu.SemaphoreType.DMA((plane, levels))],
        compiler_params=pltpu.CompilerParams(vmem_limit_bytes=8 << 20),
        cost_estimate=pl.CostEstimate(flops=0, bytes_accessed=8 * levels * plane * lines * bins, transcendentals=0),
        name="regroup",
    )(*received)


def azimuth_tables(taps_ref, table):
    length = taps_ref.shape[1]
    diagonals = table.shape[2]
    for part in range(2):
        row = jnp.concatenate(
            [jnp.zeros((1, BLOCK), jnp.float32), taps_ref[part : part + 1, :]], axis=1
        )
        full = toeplitz(row, BLOCK, length + 2 * BLOCK)
        for diagonal in range(diagonals):
            at = (diagonal + 1) * BLOCK
            table[part, 0, diagonal], table[part, 1, diagonal] = split(full[:, at : at + BLOCK])


def azimuth_sums(table, lines_ref):
    diagonals = table.shape[2]
    middle = diagonals // 2
    blocks = lines_ref.shape[0] // BLOCK
    pieces = [split(lines_ref[b * BLOCK : (b + 1) * BLOCK, :]) for b in range(blocks)]
    for b in range(blocks):
        at = slice(b * BLOCK, (b + 1) * BLOCK)
        for part in range(2):
            sums = None
            for diagonal in range(diagonals):
                other = b + diagonal - middle
                if not 0 <= other < blocks:
                    continue
                m_high, m_low = pieces[other]
                t_high, t_low = table[part, 0, diagonal], table[part, 1, diagonal]
                for left, right in ((t_high, m_high), (t_high, m_low), (t_low, m_high)):
                    term = lax.dot_general(left, right, PLAIN, preferred_element_type=jnp.float32)
                    sums = term if sums is None else sums + term
            yield part, at, sums


def azimuth_first(planes, *refs):
    outer, levels, inner = planes
    taps_ref, *sources, out_ref, table, lines_ref, sems = refs
    lines = sources[0].shape[1]
    level = lax.axis_index("gy") // inner
    place = lax.axis_index("gx") * inner + lax.rem(lax.axis_index("gy"), inner)
    copies = []
    for q, source in enumerate(sources):
        other = place ^ q
        for k in range(levels):
            device = ((other // inner) * levels + (level ^ k)) * inner + lax.rem(other, inner)
            rows = pl.ds(pl.multiple_of(device * lines, lines), lines)
            copies.append(pltpu.make_async_copy(source.at[k], lines_ref.at[rows], sems.at[q, k]))
            copies[-1].start()
    for copy in copies:
        copy.wait()
    azimuth_tables(taps_ref, table)
    for part, at, sums in azimuth_sums(table, lines_ref):
        out_ref[part, at, :] = sums if part == 0 else 0.0 - sums


def azimuth_second(taps_ref, lines_ref, earlier_ref, out_ref, table):
    azimuth_tables(taps_ref, table)
    for part, at, sums in azimuth_sums(table, lines_ref):
        out_ref[1 - part, at, :] = earlier_ref[1 - part, at, :] + sums


def azimuth_call(azimuth_ref, lines, planes, earlier=None):
    outer, levels, inner = planes
    bins = lines[0].shape[-1]
    count = sum(array.size for array in lines) // bins
    diagonals = azimuth_ref.shape[1] // BLOCK + 1
    vmem = pl.BlockSpec(memory_space=pltpu.VMEM)
    scratch = [pltpu.VMEM((2, 2, diagonals, BLOCK, BLOCK), jnp.bfloat16)]
    if earlier is None:
        kernel = functools.partial(azimuth_first, planes)
        operands = [azimuth_ref, *lines]
        in_specs = [vmem] + [pl.BlockSpec(memory_space=pl.ANY)] * len(lines)
        scratch += [pltpu.VMEM((count, bins), jnp.float32), pltpu.SemaphoreType.DMA((outer * inner, levels))]
    else:
        kernel = azimuth_second
        operands = [azimuth_ref, lines[0].reshape(count, bins), earlier]
        in_specs = [vmem] * 3
    return pl.pallas_call(
        kernel,
        out_shape=jax.ShapeDtypeStruct((2, count, bins), jnp.float32),
        in_specs=in_specs,
        out_specs=vmem,
        scratch_shapes=scratch,
        compiler_params=pltpu.CompilerParams(vmem_limit_bytes=40 << 20),
        cost_estimate=pl.CostEstimate(
            flops=20 * 2 * 3 * 2 * count * BLOCK * bins, bytes_accessed=4 * 3 * count * bins, transcendentals=0
        ),
        name="azimuth_" + ("first" if earlier is None else "second"),
    )(*operands)


def pairs_of(planes, level_step, place_step):
    outer, levels, inner = planes
    pairs = []
    for device in range(outer * levels * inner):
        place = (device // (levels * inner)) * inner + device % inner
        level = (device // inner) % levels
        place, level = place ^ place_step, level ^ level_step
        pairs.append((device, ((place // inner) * levels + level) * inner + place % inner))
    return pairs


def per_device(echoes, range_ref, azimuth_ref, shift_bins, interp_weights):
    outer, level_all = lax.axis_size("gx"), lax.axis_size("gy")
    levels = LEVELS
    planes = (outer, levels, level_all // levels)
    inputs = (echoes, range_ref, shift_bins, interp_weights)
    by_level = range_call(0, *inputs, planes)
    *by_level, shift_later = lax.optimization_barrier((*by_level, shift_bins))
    later = (echoes, range_ref, shift_later, interp_weights)
    received = [by_level[0]] + [
        lax.ppermute(by_level[k], AXES, pairs_of(planes, k, 0)) for k in range(1, levels)
    ]
    migrated = range_call(1, *later, planes)
    moved = lax.all_to_all(migrated, AXES, split_axis=0, concat_axis=0, tiled=True)
    *received, migrated = lax.optimization_barrier((*received, migrated))
    by_place = regroup_call(received)
    first = [by_place[0]] + [
        lax.ppermute(by_place[q], AXES, pairs_of(planes, 0, q)) for q in range(1, planes[0] * planes[2])
    ]
    image = azimuth_call(azimuth_ref, first, planes)
    return azimuth_call(azimuth_ref, [moved], planes, image)


def solution(mesh):
    placed = (P(None, AXES, None), P(), P(), P(AXES), P(AXES, None))
    return jax.shard_map(
        per_device,
        mesh=mesh,
        in_specs=placed,
        out_specs=P(None, None, AXES),
        check_vma=False,
    )
```

```python
import functools

import jax
import jax.numpy as jnp
from jax import lax
from jax.experimental import pallas as pl
from jax.experimental.pallas import tpu as pltpu
from jax.sharding import PartitionSpec as P

TAPS = 8
BLOCK = 256
LANE = 128
AXES = ("gx", "gy")
CORES = 2
LEVELS = 4
AHEAD = 10

ROWS_BY_ROWS = (((1,), (1,)), ((), ()))
PLAIN = (((1,), (0,)), ((), ()))


def split(values):
    high = values.astype(jnp.bfloat16)
    return high, (values - high.astype(jnp.float32)).astype(jnp.bfloat16)


def toeplitz(row, rows, width):
    row = jnp.concatenate([row, jnp.zeros((1, width - row.shape[1]), jnp.float32)], axis=1)
    return pltpu.roll(jnp.broadcast_to(row, (rows, width)), 0, axis=1, stride=1, stride_axis=0)


def range_kernel(own, planes, lines, blocks, sections, shift_ref, taps_hbm, weights_hbm, echoes_hbm, *refs):
    if own:
        *outs, taps_ref, weights_ref, echoes_ref, even, odd, table, compressed, sems, ready, out_sems = refs
    else:
        ready, taps_ref, weights_ref, echoes_ref, even, odd, table, compressed, sems = refs
    segments, levels, inner = planes
    core = lax.rem(lax.axis_index("gx"), CORES)
    width = blocks // (CORES * segments)
    halo = (sections - 1) // 2 + 1
    span = width + 2 * halo

    def lanes(block, count):
        return pl.ds(pl.multiple_of(block * BLOCK, BLOCK), count * BLOCK)

    copies = [
        pltpu.make_async_copy(taps_hbm, taps_ref, sems.at[0]),
        pltpu.make_async_copy(weights_hbm, weights_ref, sems.at[1]),
    ]
    for segment in range(segments):
        first = (CORES * segment + core) * width
        moves = (
            (jnp.maximum(first - halo, 0), 0, halo),
            (first, halo, width),
            (jnp.minimum(first + width, blocks - halo), halo + width, halo),
        )
        for n, (source, to, count) in enumerate(moves):
            target = echoes_ref.at[segment, :, :, to * BLOCK : (to + count) * BLOCK]
            copies.append(
                pltpu.make_async_copy(
                    echoes_hbm.at[:, :, lanes(source, count)], target, sems.at[2 + 3 * segment + n]
                )
            )
    for copy in copies:
        copy.start()
    copies[0].wait()
    copies[1].wait()
    real = toeplitz(taps_ref[0:1, :], BLOCK, sections * BLOCK)
    imag = toeplitz(taps_ref[1:2, :], BLOCK, sections * BLOCK)
    for kind, values in enumerate((real, imag, real - imag)):
        table[kind, 0], table[kind, 1] = split(values)
    for copy in copies[2:]:
        copy.wait()
    at_start, at_end = core == 0, core == CORES - 1

    def piece(segment, part, block):
        values = echoes_ref[segment, part, :, block * BLOCK : (block + 1) * BLOCK]
        if segment == 0 and block < halo:
            values = jnp.where(at_start, 0.0, values)
        if segment == segments - 1 and block >= halo + width:
            values = jnp.where(at_end, 0.0, values)
        return values

    for segment in range(segments):
        for offset, ref in ((0, even), (1, odd)):
            for pair in range((span - offset) // 2):
                first = 2 * pair + offset
                parts = [
                    jnp.concatenate([piece(segment, part, first), piece(segment, part, first + 1)], axis=0)
                    for part in range(2)
                ]
                at = slice((segment * span + 2 * pair) * lines, (segment * span + 2 * pair + 2) * lines)
                for kind, values in enumerate((parts[0], parts[1], parts[0] + parts[1])):
                    ref[kind, 0, at, :], ref[kind, 1, at, :] = split(values)
    rows = (width + 2) * lines
    products = []
    for kind in range(3):
        sums = None
        for section in range(sections):
            ref = even if section % 2 == 0 else odd
            starts = [(segment * span + section - section % 2) * lines for segment in range(segments)]
            x_high, x_low = [
                jnp.concatenate([ref[kind, which, start : start + rows, :] for start in starts], axis=0)
                for which in range(2)
            ]
            at = slice(section * BLOCK, (section + 1) * BLOCK)
            t_high, t_low = table[kind, 0, :, at], table[kind, 1, :, at]
            for left, right in ((x_high, t_high), (x_low, t_high), (x_high, t_low)):
                term = lax.dot_general(left, right, ROWS_BY_ROWS, preferred_element_type=jnp.float32)
                sums = term if sums is None else sums + term
        products.append(sums)
    compressed[0] = products[0] + products[1]
    compressed[1] = products[2] - products[0] + products[1]
    for part in range(2):
        low, high = slice(0, lines), slice(segments * rows - lines, segments * rows)
        compressed[part, low, :] = jnp.where(at_start, 0.0, compressed[part, low, :])
        compressed[part, high, :] = jnp.where(at_end, 0.0, compressed[part, high, :])
    migrate(lines, segments, width, shift_ref, weights_ref, compressed, ready)
    if own:
        mine = lax.axis_index("gy") // inner
        sends = []
        for k, out in enumerate(outs):
            sends.append(pltpu.make_async_copy(ready.at[:, mine ^ k], out, out_sems.at[k]))
            sends[-1].start()
        for send in sends:
            send.wait()


def place_of(device, shape):
    at = []
    for extent in reversed(shape[:-2]):
        at.insert(0, device % extent)
        device //= extent
    return at


def migrate(lines, segments, width, shift_ref, weights_ref, compressed, out_ref):
    per = out_ref.shape[-1] // LANE
    lane = lax.broadcasted_iota(jnp.int32, (lines, LANE), 1)
    row = lax.broadcasted_iota(jnp.int32, (lines, LANE), 0)
    shift = jnp.zeros((lines, LANE), jnp.int32)
    for line in range(lines):
        shift = jnp.where(row == line, shift_ref[line], shift)
    places = [lane + shift - (TAPS // 2 - 1) + step for step in range(2)]
    index = [place & (LANE - 1) for place in places]
    before = [place < 0 for place in places]
    after = [place >= LANE for place in places]
    weight = [jnp.broadcast_to(weights_ref[:, j : j + 1], (lines, LANE)) for j in range(TAPS)]
    inside = lane < LANE - 2
    tiles = width * BLOCK // LANE
    first = BLOCK // LANE

    for segment in range(segments):
        for part in range(2):

            def turned(tile, step):
                block = segment * (width + 2) + (tile + first) * LANE // BLOCK
                at = ((tile + first) * LANE) % BLOCK
                values = compressed[part, block * lines : (block + 1) * lines, at : at + LANE]
                return jnp.take_along_axis(values, index[step], axis=1, mode="promise_in_bounds")

            later = [turned(tiles + 1, step) for step in range(2)]
            here = [turned(tiles, step) for step in range(2)]
            carried = [jnp.zeros((lines, LANE), jnp.float32)] * 3
            for tile in range(tiles, -1, -1):
                earlier = [turned(tile - 1, step) for step in range(2)]
                pair = [
                    jnp.where(before[step], earlier[step], jnp.where(after[step], later[step], here[step]))
                    for step in range(2)
                ]
                total = None
                for k in (3, 2, 1, 0):
                    term = weight[2 * k] * pair[0] + weight[2 * k + 1] * pair[1]
                    if total is None:
                        total = term
                    else:
                        rolled = pltpu.roll(total, LANE - 2, axis=1)
                        total = jnp.where(inside, rolled, carried[k]) + term
                        carried[k] = rolled
                if tile < tiles:
                    place = place_of(segment * (tiles // per) + tile // per, out_ref.shape)
                    at = (tile % per) * LANE
                    out_ref[(*place, slice(part * lines, (part + 1) * lines), slice(at, at + LANE))] = total
                later, here = here, earlier


def range_call(own, echoes, range_ref, shift_bins, weights, planes):
    lines, range_total = echoes.shape[1], echoes.shape[2]
    blocks = range_total // BLOCK
    sections = range_ref.shape[1] // BLOCK + 1
    segments, levels, inner = planes
    bins = range_total // (CORES * segments * levels * inner)
    width = blocks // (CORES * segments)
    span = width + sections + 1
    flops = 2 * 3 * 3 * segments * (width + 2) * lines * sections * BLOCK * BLOCK
    scratch = [
        pltpu.VMEM(range_ref.shape, jnp.float32),
        pltpu.VMEM(weights.shape, jnp.float32),
        pltpu.VMEM((segments, 2, lines, span * BLOCK), jnp.float32),
        pltpu.VMEM((3, 2, segments * span * lines, BLOCK), jnp.bfloat16),
        pltpu.VMEM((3, 2, segments * span * lines, BLOCK), jnp.bfloat16),
        pltpu.VMEM((3, 2, BLOCK, sections * BLOCK), jnp.bfloat16),
        pltpu.VMEM((2, segments * (width + 2) * lines, BLOCK), jnp.float32),
        pltpu.SemaphoreType.DMA((2 + 3 * segments,)),
    ]
    if own:
        out_shape = [jax.ShapeDtypeStruct((segments, inner, 2 * lines, bins), jnp.float32)] * levels
        out_specs = [pl.BlockSpec(memory_space=pltpu.HBM)] * levels
        scratch += [
            pltpu.VMEM((segments, levels, inner, 2 * lines, bins), jnp.float32),
            pltpu.SemaphoreType.DMA((levels,)),
        ]
    else:
        out_shape = jax.ShapeDtypeStruct((segments * levels * inner, 2 * lines, bins), jnp.float32)
        out_specs = pl.BlockSpec(memory_space=pltpu.VMEM)
    return pl.pallas_call(
        functools.partial(range_kernel, own, planes, lines, blocks, sections),
        out_shape=out_shape,
        in_specs=[pl.BlockSpec(memory_space=pltpu.SMEM)] + [pl.BlockSpec(memory_space=pltpu.HBM if own else pl.ANY)] * 3,
        out_specs=out_specs,
        scratch_shapes=scratch,
        compiler_params=pltpu.CompilerParams(vmem_limit_bytes=(60 if own else 40) << 20),
        cost_estimate=pl.CostEstimate(flops=flops, bytes_accessed=3 * echoes.size * 2, transcendentals=0),
        name="range_own" if own else "range_partner",
    )(shift_bins, range_ref, weights, echoes)


def regroup_kernel(levels, plane, *refs):
    sources, outs, sems = refs[:levels], refs[levels:-1], refs[-1]
    inner = sources[0].shape[1]
    mine = place_here(inner)
    copies = []
    for q in range(plane):
        place = mine ^ q
        for k in range(levels):
            source = sources[k].at[place // inner, lax.rem(place, inner)]
            copies.append(pltpu.make_async_copy(source, outs[q].at[k], sems.at[q, k]))
            copies[-1].start()
    for copy in copies:
        copy.wait()


def place_here(inner):
    return (lax.axis_index("gx") // CORES) * inner + lax.rem(lax.axis_index("gy"), inner)


def regroup_call(received):
    levels = len(received)
    segments, inner, rows, bins = received[0].shape
    plane = segments * inner
    return pl.pallas_call(
        functools.partial(regroup_kernel, levels, plane),
        out_shape=[jax.ShapeDtypeStruct((levels, rows, bins), jnp.float32)] * plane,
        in_specs=[pl.BlockSpec(memory_space=pl.ANY)] * levels,
        out_specs=[pl.BlockSpec(memory_space=pltpu.HBM)] * plane,
        scratch_shapes=[pltpu.SemaphoreType.DMA((plane, levels))],
        compiler_params=pltpu.CompilerParams(vmem_limit_bytes=8 << 20),
        cost_estimate=pl.CostEstimate(flops=0, bytes_accessed=8 * levels * plane * rows * bins, transcendentals=0),
        name="regroup",
    )(*received)


def azimuth_tables(taps_ref, table):
    length = taps_ref.shape[1]
    diagonals = table.shape[2]
    for part in range(2):
        row = jnp.concatenate(
            [jnp.zeros((1, BLOCK), jnp.float32), taps_ref[part : part + 1, :]], axis=1
        )
        full = toeplitz(row, BLOCK, length + 2 * BLOCK)
        for diagonal in range(diagonals):
            at = (diagonal + 1) * BLOCK
            table[part, 0, diagonal], table[part, 1, diagonal] = split(full[:, at : at + BLOCK])


def azimuth_sums(table, lines_ref):
    diagonals = table.shape[2]
    middle = diagonals // 2
    blocks = lines_ref.shape[1] // BLOCK
    pieces = [
        [split(lines_ref[part, b * BLOCK : (b + 1) * BLOCK, :]) for b in range(blocks)] for part in range(2)
    ]

    def product(b, taps, part):
        sums = None
        for diagonal in range(diagonals):
            other = b + diagonal - middle
            if not 0 <= other < blocks:
                continue
            m_high, m_low = pieces[part][other]
            t_high, t_low = table[taps, 0, diagonal], table[taps, 1, diagonal]
            for left, right in ((t_high, m_high), (t_high, m_low), (t_low, m_high)):
                term = lax.dot_general(left, right, PLAIN, preferred_element_type=jnp.float32)
                sums = term if sums is None else sums + term
        return sums

    for b in range(blocks):
        at = slice(b * BLOCK, (b + 1) * BLOCK)
        yield 0, at, product(b, 0, 0) + product(b, 1, 1)
        yield 1, at, product(b, 0, 1) - product(b, 1, 0)


def clear_other(lines_ref, segments, core):
    run = lines_ref.shape[1] // (CORES * segments)
    for segment in range(segments):
        rows = pl.ds(pl.multiple_of((CORES * segment + 1 - core) * run, run), run)
        for part in range(2):
            lines_ref[part, rows, :] = jnp.zeros((run, lines_ref.shape[2]), jnp.float32)


def azimuth_first(planes, *refs):
    segments, levels, inner = planes
    taps_ref, *sources, out_ref, table, lines_ref, sems = refs
    lines = sources[0].shape[1] // 2
    core = lax.rem(lax.axis_index("gx"), CORES)
    level = lax.axis_index("gy") // inner
    mine = place_here(inner)
    copies = []
    for q, source in enumerate(sources):
        place = mine ^ q
        for k in range(levels):
            device = (((place // inner) * CORES + core) * levels + (level ^ k)) * inner + lax.rem(place, inner)
            rows = pl.ds(pl.multiple_of(device * lines, lines), lines)
            for part in range(2):
                copies.append(
                    pltpu.make_async_copy(
                        source.at[k, part * lines : (part + 1) * lines], lines_ref.at[part, rows], sems.at[q, k, part]
                    )
                )
                copies[-1].start()
    clear_other(lines_ref, segments, core)
    for copy in copies:
        copy.wait()
    azimuth_tables(taps_ref, table)
    for part, at, sums in azimuth_sums(table, lines_ref):
        out_ref[part, at, :] = sums


def azimuth_second(planes, table, moved_ref, earlier_ref, out_ref, lines_ref):
    segments, levels, inner = planes
    lines = moved_ref.shape[1] // 2
    run = levels * inner * lines
    core = lax.rem(lax.axis_index("gx"), CORES)
    clear_other(lines_ref, segments, 1 - core)
    for segment in range(segments):
        rows = pl.ds(pl.multiple_of((CORES * segment + 1 - core) * run, run), run)
        for part in range(2):
            values = moved_ref[
                segment * levels * inner : (segment + 1) * levels * inner, part * lines : (part + 1) * lines, :
            ]
            lines_ref[part, rows, :] = values.reshape(run, values.shape[-1])
    for part, at, sums in azimuth_sums(table, lines_ref):
        out_ref[part, at, :] = earlier_ref[part, at, :] + sums


def azimuth_call(planes, count, bins, azimuth_ref, arrived=None, table=None, moved=None, earlier=None):
    segments, levels, inner = planes
    diagonals = azimuth_ref.shape[1] // BLOCK + 1
    image = jax.ShapeDtypeStruct((2, count, bins), jnp.float32)
    vmem = pl.BlockSpec(memory_space=pltpu.VMEM)
    scratch = [pltpu.VMEM((2, count, bins), jnp.float32)]
    if earlier is None:
        kernel = azimuth_first
        operands = [azimuth_ref, *arrived]
        in_specs = [vmem] + [pl.BlockSpec(memory_space=pl.ANY)] * len(arrived)
        out_shape = [image, jax.ShapeDtypeStruct((2, 2, diagonals, BLOCK, BLOCK), jnp.bfloat16)]
        out_specs = [vmem, vmem]
        scratch += [pltpu.SemaphoreType.DMA((segments * inner, levels, 2))]
        weight = AHEAD
    else:
        kernel = azimuth_second
        operands = [table, moved, earlier]
        in_specs = [vmem] * 3
        out_shape, out_specs = image, vmem
        weight = 1
    return pl.pallas_call(
        functools.partial(kernel, planes),
        out_shape=out_shape,
        in_specs=in_specs,
        out_specs=out_specs,
        scratch_shapes=scratch,
        compiler_params=pltpu.CompilerParams(vmem_limit_bytes=40 << 20),
        cost_estimate=pl.CostEstimate(
            flops=weight * 2 * 3 * 4 * count * BLOCK * bins, bytes_accessed=4 * 4 * count * bins, transcendentals=0
        ),
        name="azimuth_first" if earlier is None else "azimuth_second",
    )(*operands)


def pairs_of(planes, level_step=0, place_step=0, core_step=0):
    segments, levels, inner = planes
    pairs = []
    for device in range(CORES * segments * levels * inner):
        core = (device // (levels * inner)) % CORES
        place = (device // (CORES * levels * inner)) * inner + device % inner
        level = (device // inner) % levels
        place, level, core = place ^ place_step, level ^ level_step, core ^ core_step
        pairs.append((device, (((place // inner) * CORES + core) * levels + level) * inner + place % inner))
    return pairs


def per_device(echoes, range_ref, azimuth_ref, shift_bins, interp_weights):
    outer, run = lax.axis_size("gx"), lax.axis_size("gy")
    segments, levels = outer // CORES, LEVELS
    planes = (segments, levels, run // levels)
    devices_all = outer * run
    bins = echoes.shape[2] // devices_all
    partner = [
        lax.ppermute(array, AXES, pairs_of(planes, core_step=1)) for array in (echoes, shift_bins, interp_weights)
    ]
    by_level = range_call(True, echoes, range_ref, shift_bins, interp_weights, planes)
    received = [by_level[0]] + [
        lax.ppermute(by_level[k], AXES, pairs_of(planes, level_step=k)) for k in range(1, levels)
    ]
    *by_level, taps_later = lax.optimization_barrier((*by_level, range_ref))
    migrated = range_call(False, partner[0], taps_later, partner[1], partner[2], planes)
    groups = [
        [(segment * CORES + core) * run + at for segment in range(segments) for at in range(run)]
        for core in range(CORES)
    ]
    moved = lax.all_to_all(migrated, AXES, split_axis=0, concat_axis=0, axis_index_groups=groups, tiled=True)
    *received, migrated = lax.optimization_barrier((*received, migrated))
    by_place = regroup_call(received)
    arrived = [by_place[0]] + [
        lax.ppermute(by_place[q], AXES, pairs_of(planes, place_step=q)) for q in range(1, len(by_place))
    ]
    count = devices_all * echoes.shape[1]
    image, table = azimuth_call(planes, count, bins, azimuth_ref, arrived)
    return azimuth_call(planes, count, bins, azimuth_ref, table=table, moved=moved, earlier=image)


def solution(mesh):
    placed = (P(None, AXES, None), P(), P(), P(AXES), P(AXES, None))
    return jax.shard_map(
        per_device,
        mesh=mesh,
        in_specs=placed,
        out_specs=P(None, None, AXES),
        check_vma=False,
    )
```

```python
import functools

import jax
import jax.numpy as jnp
from jax import lax
from jax.experimental import pallas as pl
from jax.experimental.pallas import tpu as pltpu
from jax.sharding import PartitionSpec as P

TAPS = 8
BLOCK = 256
LANE = 128
AXES = ("gx", "gy")
CORES = 2
LEVELS = 4
AHEAD = 10

ROWS_BY_ROWS = (((1,), (1,)), ((), ()))
PLAIN = (((1,), (0,)), ((), ()))


def split(values):
    high = values.astype(jnp.bfloat16)
    return high, (values - high.astype(jnp.float32)).astype(jnp.bfloat16)


def toeplitz(row, rows, width):
    if width > row.shape[1]:
        row = jnp.concatenate([row, jnp.zeros((1, width - row.shape[1]), jnp.float32)], axis=1)
    return pltpu.roll(jnp.broadcast_to(row, (rows, width)), 0, axis=1, stride=1, stride_axis=0)


def range_kernel(own, planes, lines, blocks, sections, *refs):
    if own:
        shift_ref, taps_hbm, weights_hbm, echoes_hbm, *outs, table, taps_ref, weights_ref, echoes_ref, even, odd, compressed, sems = refs
    else:
        shift_ref, table, weights_ref, echoes_ref, out_ref, even, odd, compressed = refs
    segments, levels, inner = planes
    core = lax.rem(lax.axis_index("gx"), CORES)
    width = blocks // (CORES * segments)
    halo = (sections - 1) // 2
    span = width + 2 + 2 * halo
    at_start, at_end = core == 0, core == CORES - 1
    if own:
        copies = [
            pltpu.make_async_copy(taps_hbm, taps_ref, sems.at[0]),
            pltpu.make_async_copy(weights_hbm, weights_ref, sems.at[1]),
            pltpu.make_async_copy(echoes_hbm, echoes_ref, sems.at[2]),
        ]
        for copy in copies:
            copy.start()
        copies[0].wait()
        copies[1].wait()
        real = toeplitz(taps_ref[0:1, :], BLOCK, sections * BLOCK)
        imag = toeplitz(taps_ref[1:2, :], BLOCK, sections * BLOCK)
        for kind, values in enumerate((real, imag, real - imag)):
            table[kind, 0], table[kind, 1] = split(values)
        copies[2].wait()

    def piece(segment, part, block):
        at = (CORES * segment + core) * width + block - halo - 1
        low = segment == 0 and block <= halo
        high = segment == segments - 1 and block > halo + width
        if low:
            at = jnp.maximum(at, 0)
        if high:
            at = jnp.minimum(at, blocks - 1)
        values = echoes_ref[part, :, pl.ds(pl.multiple_of(at * BLOCK, BLOCK), BLOCK)]
        if low:
            values = jnp.where(at_start, 0.0, values)
        if high:
            values = jnp.where(at_end, 0.0, values)
        return values

    for segment in range(segments):
        for offset, ref in ((0, even), (1, odd)):
            for pair in range((span - offset) // 2):
                first = 2 * pair + offset
                parts = [
                    jnp.concatenate([piece(segment, part, first), piece(segment, part, first + 1)], axis=0)
                    for part in range(2)
                ]
                at = slice((segment * span + 2 * pair) * lines, (segment * span + 2 * pair + 2) * lines)
                for kind, values in enumerate((parts[0], parts[1], parts[0] + parts[1])):
                    ref[kind, 0, at, :], ref[kind, 1, at, :] = split(values)
    rows = (width + 2) * lines
    products = []
    for kind in range(3):
        sums = None
        for section in range(sections):
            ref = even if section % 2 == 0 else odd
            starts = [(segment * span + section - section % 2) * lines for segment in range(segments)]
            x_high, x_low = [
                jnp.concatenate([ref[kind, which, start : start + rows, :] for start in starts], axis=0)
                for which in range(2)
            ]
            at = slice(section * BLOCK, (section + 1) * BLOCK)
            t_high, t_low = table[kind, 0, :, at], table[kind, 1, :, at]
            for left, right in ((x_high, t_high), (x_low, t_high), (x_high, t_low)):
                term = lax.dot_general(left, right, ROWS_BY_ROWS, preferred_element_type=jnp.float32)
                sums = term if sums is None else sums + term
        products.append(sums)
    compressed[0] = products[0] + products[1]
    compressed[1] = products[2] - products[0] + products[1]
    for part in range(2):
        low, high = slice(0, lines), slice(segments * rows - lines, segments * rows)
        compressed[part, low, :] = jnp.where(at_start, 0.0, compressed[part, low, :])
        compressed[part, high, :] = jnp.where(at_end, 0.0, compressed[part, high, :])

    run = width // levels
    for segment in range(segments):
        for step in range(levels):
            level = (lax.axis_index("gy") // inner) ^ step if own else step
            first = (segment * (width + 2) + 1 + level * run) * lines
            for part in range(2):

                def load(tile):
                    block, at = tile * LANE // BLOCK, tile * LANE % BLOCK
                    start = first + block * lines
                    if own:
                        start = pl.multiple_of(start, lines)
                    return compressed[part, pl.ds(start, lines), at : at + LANE]

                moved = migrate(lines, run * BLOCK // LANE, shift_ref, weights_ref, load)
                for tile, values in enumerate(moved):
                    rows_at = slice(part * lines, (part + 1) * lines)
                    if own:
                        per = outs[step].shape[-1] // LANE
                        at = (tile % per) * LANE
                        outs[step][segment, tile // per, rows_at, at : at + LANE] = values
                    else:
                        per = out_ref.shape[-1] // LANE
                        at = (tile % per) * LANE
                        place = (segment * levels + step) * inner + tile // per
                        out_ref[place, rows_at, at : at + LANE] = values


def migrate(lines, tiles, shift_ref, weights_ref, load):
    lane = lax.broadcasted_iota(jnp.int32, (lines, LANE), 1)
    row = lax.broadcasted_iota(jnp.int32, (lines, LANE), 0)
    shift = jnp.zeros((lines, LANE), jnp.int32)
    for line in range(lines):
        shift = jnp.where(row == line, shift_ref[line], shift)
    inside = lane < LANE - 2
    pairs = []
    for step in range(2):
        place = lane + shift - (TAPS // 2 - 1) + step
        index = place & (LANE - 1)
        turned = [
            jnp.take_along_axis(load(tile), index, axis=1, mode="promise_in_bounds") for tile in range(-1, tiles + 2)
        ]
        pairs.append(
            [
                jnp.where(place < 0, turned[tile], jnp.where(place >= LANE, turned[tile + 2], turned[tile + 1]))
                for tile in range(tiles + 1)
            ]
        )
    totals = None
    for k in (3, 2, 1, 0):
        even, odd = [jnp.broadcast_to(weights_ref[:, 2 * k + n : 2 * k + n + 1], (lines, LANE)) for n in range(2)]
        terms = [even * first + odd * second for first, second in zip(*pairs)]
        if totals is None:
            totals = terms
        else:
            rolled = [pltpu.roll(total, LANE - 2, axis=1) for total in totals]
            rolled.append(jnp.zeros((lines, LANE), jnp.float32))
            totals = [
                jnp.where(inside, rolled[tile], rolled[tile + 1]) + terms[tile] for tile in range(tiles + 1)
            ]
    return totals[:tiles]


def range_call(own, echoes, taps, shift_bins, weights, planes):
    lines, range_total = echoes.shape[1], echoes.shape[2]
    blocks = range_total // BLOCK
    sections = (taps.shape[1] if own else taps.shape[-1] - BLOCK) // BLOCK + 1
    segments, levels, inner = planes
    bins = range_total // (CORES * segments * levels * inner)
    width = blocks // (CORES * segments)
    span = width + sections + 1
    flops = 2 * 3 * 3 * segments * (width + 2) * lines * sections * BLOCK * BLOCK
    vmem, hbm = pl.BlockSpec(memory_space=pltpu.VMEM), pl.BlockSpec(memory_space=pltpu.HBM)
    scratch = [
        pltpu.VMEM((3, 2, segments * span * lines, BLOCK), jnp.bfloat16),
        pltpu.VMEM((3, 2, segments * span * lines, BLOCK), jnp.bfloat16),
        pltpu.VMEM((2, segments * (width + 2) * lines, BLOCK), jnp.float32),
    ]
    operands = [shift_bins, taps, weights, echoes]
    if own:
        operands = [pltpu.with_memory_space_constraint(array, pltpu.HBM) for array in operands]
        in_specs = [pl.BlockSpec(memory_space=pltpu.SMEM), hbm, hbm, hbm]
        out_shape = [jax.ShapeDtypeStruct((segments, inner, 2 * lines, bins), jnp.float32)] * levels
        out_shape += [jax.ShapeDtypeStruct((3, 2, BLOCK, sections * BLOCK), jnp.bfloat16)]
        out_specs = [vmem] * (levels + 1)
        scratch = [
            pltpu.VMEM(taps.shape, jnp.float32),
            pltpu.VMEM(weights.shape, jnp.float32),
            pltpu.VMEM(echoes.shape, jnp.float32),
            *scratch,
            pltpu.SemaphoreType.DMA((3,)),
        ]
    else:
        in_specs = [pl.BlockSpec(memory_space=pltpu.SMEM), vmem, vmem, vmem]
        out_shape = jax.ShapeDtypeStruct((segments * levels * inner, 2 * lines, bins), jnp.float32)
        out_specs = vmem
    return pl.pallas_call(
        functools.partial(range_kernel, own, planes, lines, blocks, sections),
        out_shape=out_shape,
        in_specs=in_specs,
        out_specs=out_specs,
        scratch_shapes=scratch,
        compiler_params=pltpu.CompilerParams(vmem_limit_bytes=24 << 20),
        cost_estimate=pl.CostEstimate(flops=flops, bytes_accessed=3 * echoes.size * 2, transcendentals=0),
        name="range_own" if own else "range_partner",
    )(*operands)


def regroup_kernel(levels, plane, *refs):
    sources, outs, sems = refs[:levels], refs[levels:-1], refs[-1]
    inner = sources[0].shape[1]
    mine = place_here(inner)
    copies = []
    for q in range(plane):
        place = mine ^ q
        for k in range(levels):
            source = sources[k].at[place // inner, lax.rem(place, inner)]
            copies.append(pltpu.make_async_copy(source, outs[q].at[k], sems.at[q, k]))
            copies[-1].start()
    for copy in copies:
        copy.wait()


def place_here(inner):
    return (lax.axis_index("gx") // CORES) * inner + lax.rem(lax.axis_index("gy"), inner)


def regroup_call(received):
    levels = len(received)
    segments, inner, rows, bins = received[0].shape
    plane = segments * inner
    return pl.pallas_call(
        functools.partial(regroup_kernel, levels, plane),
        out_shape=[jax.ShapeDtypeStruct((levels, rows, bins), jnp.float32)] * plane,
        in_specs=[pl.BlockSpec(memory_space=pl.ANY)] * levels,
        out_specs=[pl.BlockSpec(memory_space=pltpu.HBM)] * plane,
        scratch_shapes=[pltpu.SemaphoreType.DMA((plane, levels))],
        compiler_params=pltpu.CompilerParams(vmem_limit_bytes=8 << 20),
        cost_estimate=pl.CostEstimate(flops=0, bytes_accessed=8 * levels * plane * rows * bins, transcendentals=0),
        name="regroup",
    )(*received)


def azimuth_tables(taps_ref, table):
    length = taps_ref.shape[1]
    diagonals = table.shape[2]
    first = (length // BLOCK + 1 - diagonals) // 2
    zeros = jnp.zeros((1, BLOCK), jnp.float32)
    for part in range(2):
        row = jnp.concatenate([zeros, taps_ref[part : part + 1, :], zeros], axis=1)
        width = (diagonals + 1) * BLOCK
        full = toeplitz(row[:, first * BLOCK : first * BLOCK + width], BLOCK, width)
        for n in range(diagonals):
            at = (n + 1) * BLOCK
            table[part, 0, n], table[part, 1, n] = split(full[:, at : at + BLOCK])


def azimuth_sums(table, lines_ref):
    diagonals = table.shape[2]
    middle = diagonals // 2
    blocks = lines_ref.shape[1] // BLOCK
    pieces = [
        [split(lines_ref[part, b * BLOCK : (b + 1) * BLOCK, :]) for b in range(blocks)] for part in range(2)
    ]

    def product(b, taps, part):
        sums = None
        for diagonal in range(diagonals):
            other = b + diagonal - middle
            if not 0 <= other < blocks:
                continue
            m_high, m_low = pieces[part][other]
            t_high, t_low = table[taps, 0, diagonal], table[taps, 1, diagonal]
            for left, right in ((t_high, m_high), (t_high, m_low), (t_low, m_high)):
                term = lax.dot_general(left, right, PLAIN, preferred_element_type=jnp.float32)
                sums = term if sums is None else sums + term
        return sums

    for b in range(blocks):
        at = slice(b * BLOCK, (b + 1) * BLOCK)
        yield 0, at, product(b, 0, 0) + product(b, 1, 1)
        yield 1, at, product(b, 0, 1) - product(b, 1, 0)


def clear_other(lines_ref, segments, core):
    run = lines_ref.shape[1] // (CORES * segments)
    for segment in range(segments):
        rows = pl.ds(pl.multiple_of((CORES * segment + 1 - core) * run, run), run)
        for part in range(2):
            lines_ref[part, rows, :] = jnp.zeros((run, lines_ref.shape[2]), jnp.float32)


def azimuth_first(planes, *refs):
    segments, levels, inner = planes
    taps_ref, *sources, out_ref, table, lines_ref, sems = refs
    lines = sources[0].shape[1] // 2
    core = lax.rem(lax.axis_index("gx"), CORES)
    level = lax.axis_index("gy") // inner
    mine = place_here(inner)
    copies = []
    for q, source in enumerate(sources):
        place = mine ^ q
        for k in range(levels):
            device = (((place // inner) * CORES + core) * levels + (level ^ k)) * inner + lax.rem(place, inner)
            rows = pl.ds(pl.multiple_of(device * lines, lines), lines)
            for part in range(2):
                copies.append(
                    pltpu.make_async_copy(
                        source.at[k, part * lines : (part + 1) * lines], lines_ref.at[part, rows], sems.at[q, k, part]
                    )
                )
                copies[-1].start()
    clear_other(lines_ref, segments, core)
    for copy in copies:
        copy.wait()
    azimuth_tables(taps_ref, table)
    for part, at, sums in azimuth_sums(table, lines_ref):
        out_ref[part, at, :] = sums


def azimuth_second(planes, table, moved_ref, earlier_ref, out_ref, lines_ref):
    segments, levels, inner = planes
    lines = moved_ref.shape[1] // 2
    run = levels * inner * lines
    core = lax.rem(lax.axis_index("gx"), CORES)
    clear_other(lines_ref, segments, 1 - core)
    for segment in range(segments):
        rows = pl.ds(pl.multiple_of((CORES * segment + 1 - core) * run, run), run)
        for part in range(2):
            values = moved_ref[
                segment * levels * inner : (segment + 1) * levels * inner, part * lines : (part + 1) * lines, :
            ]
            lines_ref[part, rows, :] = values.reshape(run, values.shape[-1])
    for part, at, sums in azimuth_sums(table, lines_ref):
        out_ref[part, at, :] = earlier_ref[part, at, :] + sums


def azimuth_call(planes, count, bins, azimuth_ref, arrived=None, table=None, moved=None, earlier=None):
    segments, levels, inner = planes
    diagonals = min(azimuth_ref.shape[1] // BLOCK + 1, 2 * (count // BLOCK) - 1)
    image = jax.ShapeDtypeStruct((2, count, bins), jnp.float32)
    vmem = pl.BlockSpec(memory_space=pltpu.VMEM)
    scratch = [pltpu.VMEM((2, count, bins), jnp.float32)]
    if earlier is None:
        kernel = azimuth_first
        operands = [azimuth_ref, *arrived]
        in_specs = [vmem] + [pl.BlockSpec(memory_space=pl.ANY)] * len(arrived)
        out_shape = [image, jax.ShapeDtypeStruct((2, 2, diagonals, BLOCK, BLOCK), jnp.bfloat16)]
        out_specs = [vmem, vmem]
        scratch += [pltpu.SemaphoreType.DMA((segments * inner, levels, 2))]
        weight = AHEAD
    else:
        kernel = azimuth_second
        operands = [table, moved, earlier]
        in_specs = [vmem] * 3
        out_shape, out_specs = image, vmem
        weight = 1
    return pl.pallas_call(
        functools.partial(kernel, planes),
        out_shape=out_shape,
        in_specs=in_specs,
        out_specs=out_specs,
        scratch_shapes=scratch,
        compiler_params=pltpu.CompilerParams(vmem_limit_bytes=24 << 20),
        cost_estimate=pl.CostEstimate(
            flops=weight * 2 * 3 * 4 * count * BLOCK * bins, bytes_accessed=4 * 4 * count * bins, transcendentals=0
        ),
        name="azimuth_first" if earlier is None else "azimuth_second",
    )(*operands)


def pairs_of(planes, level_step=0, place_step=0, core_step=0):
    segments, levels, inner = planes
    pairs = []
    for device in range(CORES * segments * levels * inner):
        core = (device // (levels * inner)) % CORES
        place = (device // (CORES * levels * inner)) * inner + device % inner
        level = (device // inner) % levels
        place, level, core = place ^ place_step, level ^ level_step, core ^ core_step
        pairs.append((device, (((place // inner) * CORES + core) * levels + level) * inner + place % inner))
    return pairs


def per_device(echoes, range_ref, azimuth_ref, shift_bins, interp_weights):
    outer, run = lax.axis_size("gx"), lax.axis_size("gy")
    segments, levels = outer // CORES, LEVELS
    planes = (segments, levels, run // levels)
    devices_all = outer * run
    bins = echoes.shape[2] // devices_all
    partner = [
        lax.ppermute(array, AXES, pairs_of(planes, core_step=1)) for array in (echoes, shift_bins, interp_weights)
    ]
    *by_level, table = range_call(True, echoes, range_ref, shift_bins, interp_weights, planes)
    received = [by_level[0]] + [
        lax.ppermute(by_level[k], AXES, pairs_of(planes, level_step=k)) for k in range(1, levels)
    ]
    migrated = range_call(False, partner[0], table, partner[1], partner[2], planes)
    groups = [
        [(segment * CORES + core) * run + at for segment in range(segments) for at in range(run)]
        for core in range(CORES)
    ]
    moved = lax.all_to_all(migrated, AXES, split_axis=0, concat_axis=0, axis_index_groups=groups, tiled=True)
    *received, migrated = lax.optimization_barrier((*received, migrated))
    by_place = regroup_call(received)
    arrived = [by_place[0]] + [
        lax.ppermute(by_place[q], AXES, pairs_of(planes, place_step=q)) for q in range(1, len(by_place))
    ]
    count = devices_all * echoes.shape[1]
    image, table = azimuth_call(planes, count, bins, azimuth_ref, arrived)
    return azimuth_call(planes, count, bins, azimuth_ref, table=table, moved=moved, earlier=image)


def solution(mesh):
    placed = (P(None, AXES, None), P(), P(), P(AXES), P(AXES, None))
    return jax.shard_map(
        per_device,
        mesh=mesh,
        in_specs=placed,
        out_specs=P(None, None, AXES),
        check_vma=False,
    )
```

```python
import functools

import jax
import jax.numpy as jnp
from jax import lax
from jax.experimental import pallas as pl
from jax.experimental.pallas import tpu as pltpu
from jax.sharding import PartitionSpec as P

TAPS = 8
BLOCK = 256
LANE = 128
AXES = ("gx", "gy")
CORES = 2
LEVELS = 4
AHEAD = 20000

ROWS_BY_ROWS = (((1,), (1,)), ((), ()))
PLAIN = (((1,), (0,)), ((), ()))


def split(values):
    high = values.astype(jnp.bfloat16)
    return high, (values - high.astype(jnp.float32)).astype(jnp.bfloat16)


def toeplitz(row, rows, width):
    if width > row.shape[1]:
        row = jnp.concatenate([row, jnp.zeros((1, width - row.shape[1]), jnp.float32)], axis=1)
    return pltpu.roll(jnp.broadcast_to(row, (rows, width)), 0, axis=1, stride=1, stride_axis=0)


def range_kernel(own, planes, lines, blocks, sections, *refs):
    if own:
        shift_ref, taps_hbm, weights_hbm, echoes_hbm, *outs, table, taps_ref, weights_ref, echoes_ref, even, odd, compressed, sems = refs
    else:
        shift_ref, table, weights_ref, echoes_ref, out_ref, even, odd, compressed, ready, sems = refs
    segments, levels, inner = planes
    core = lax.rem(lax.axis_index("gx"), CORES)
    width = blocks // (CORES * segments)
    halo = (sections - 1) // 2
    span = width + 2 + 2 * halo
    at_start, at_end = core == 0, core == CORES - 1
    if own:
        copies = [
            pltpu.make_async_copy(taps_hbm, taps_ref, sems.at[0]),
            pltpu.make_async_copy(weights_hbm, weights_ref, sems.at[1]),
            pltpu.make_async_copy(echoes_hbm, echoes_ref, sems.at[2]),
        ]
        for copy in copies:
            copy.start()
        copies[0].wait()
        copies[1].wait()
        real = toeplitz(taps_ref[0:1, :], BLOCK, sections * BLOCK)
        imag = toeplitz(taps_ref[1:2, :], BLOCK, sections * BLOCK)
        for kind, values in enumerate((real, imag, real - imag)):
            table[kind, 0], table[kind, 1] = split(values)
        copies[2].wait()

    def piece(segment, part, block):
        at = (CORES * segment + core) * width + block - halo - 1
        low = segment == 0 and block <= halo
        high = segment == segments - 1 and block > halo + width
        if low:
            at = jnp.maximum(at, 0)
        if high:
            at = jnp.minimum(at, blocks - 1)
        values = echoes_ref[part, :, pl.ds(pl.multiple_of(at * BLOCK, BLOCK), BLOCK)]
        if low:
            values = jnp.where(at_start, 0.0, values)
        if high:
            values = jnp.where(at_end, 0.0, values)
        return values

    for segment in range(segments):
        for offset, ref in ((0, even), (1, odd)):
            for pair in range((span - offset) // 2):
                first = 2 * pair + offset
                parts = [
                    jnp.concatenate([piece(segment, part, first), piece(segment, part, first + 1)], axis=0)
                    for part in range(2)
                ]
                at = slice((segment * span + 2 * pair) * lines, (segment * span + 2 * pair + 2) * lines)
                for kind, values in enumerate((parts[0], parts[1], parts[0] + parts[1])):
                    ref[kind, 0, at, :], ref[kind, 1, at, :] = split(values)
    rows = (width + 2) * lines
    products = []
    for kind in range(3):
        sums = None
        for section in range(sections):
            ref = even if section % 2 == 0 else odd
            starts = [(segment * span + section - section % 2) * lines for segment in range(segments)]
            x_high, x_low = [
                jnp.concatenate([ref[kind, which, start : start + rows, :] for start in starts], axis=0)
                for which in range(2)
            ]
            at = slice(section * BLOCK, (section + 1) * BLOCK)
            t_high, t_low = table[kind, 0, :, at], table[kind, 1, :, at]
            for left, right in ((x_high, t_high), (x_low, t_high), (x_high, t_low)):
                term = lax.dot_general(left, right, ROWS_BY_ROWS, preferred_element_type=jnp.float32)
                sums = term if sums is None else sums + term
        products.append(sums)
    compressed[0] = products[0] + products[1]
    compressed[1] = products[2] - products[0] + products[1]
    for part in range(2):
        low, high = slice(0, lines), slice(segments * rows - lines, segments * rows)
        compressed[part, low, :] = jnp.where(at_start, 0.0, compressed[part, low, :])
        compressed[part, high, :] = jnp.where(at_end, 0.0, compressed[part, high, :])

    plan = migration_plan(lines, shift_ref, weights_ref)
    sends = []
    run = width // levels
    for step in range(levels):
        level = (lax.axis_index("gy") // inner) ^ step if own else step
        streams = [(segment, part) for segment in range(segments) for part in range(2)]

        def loader(segment, part):
            first = (segment * (width + 2) + 1 + level * run) * lines

            def load(tile):
                block, at = tile * LANE // BLOCK, tile * LANE % BLOCK
                start = first + block * lines
                if own:
                    start = pl.multiple_of(start, lines)
                return compressed[part, pl.ds(start, lines), at : at + LANE]

            return load

        moved = migrate(run * BLOCK // LANE, plan, [loader(*stream) for stream in streams])
        for (segment, part), row in zip(streams, moved):
            target = (outs[step] if own else ready.at[step]).at[segment]
            per = target.shape[-1] // LANE
            for tile, values in enumerate(row):
                at = (tile % per) * LANE
                target[tile // per, part * lines : (part + 1) * lines, at : at + LANE] = values
        if not own:
            for segment in range(segments):
                first = (segment * levels + step) * inner
                sends.append(
                    pltpu.make_async_copy(
                        ready.at[step, segment], out_ref.at[first : first + inner], sems.at[step, segment]
                    )
                )
                sends[-1].start()
    for send in sends:
        send.wait()


def migration_plan(lines, shift_ref, weights_ref):
    lane = lax.broadcasted_iota(jnp.int32, (lines, LANE), 1)
    row = lax.broadcasted_iota(jnp.int32, (lines, LANE), 0)
    shift = jnp.zeros((lines, LANE), jnp.int32)
    for line in range(lines):
        shift = jnp.where(row == line, shift_ref[line], shift)
    steps = []
    for step in range(2):
        place = lane + shift - (TAPS // 2 - 1) + step
        steps.append((place & (LANE - 1), place < 0, place >= LANE))
    weights = [jnp.broadcast_to(weights_ref[:, j : j + 1], (lines, LANE)) for j in range(TAPS)]
    return steps, weights, lane


def migrate(tiles, plan, loads):
    steps, weights, lane = plan
    pairs = []
    for index, below, above in steps:
        turned = [
            [
                jnp.take_along_axis(load(tile), index, axis=1, mode="promise_in_bounds")
                for tile in range(-1, tiles + 2)
            ]
            for load in loads
        ]
        pairs.append(
            [
                [
                    jnp.where(below, row[tile], jnp.where(above, row[tile + 2], row[tile + 1]))
                    for tile in range(tiles + 1)
                ]
                for row in turned
            ]
        )
    totals = None
    for k in range(TAPS // 2):
        terms = [
            [weights[2 * k] * one + weights[2 * k + 1] * two for one, two in zip(*rows)] for rows in zip(*pairs)
        ]
        if k == 0:
            totals = [row[:tiles] for row in terms]
            continue
        rolled = [[pltpu.roll(term, LANE - 2 * k, axis=1) for term in row] for row in terms]
        inside = lane < LANE - 2 * k
        totals = [
            [total[tile] + jnp.where(inside, row[tile], row[tile + 1]) for tile in range(tiles)]
            for total, row in zip(totals, rolled)
        ]
    return totals


def range_call(own, echoes, taps, shift_bins, weights, planes):
    lines, range_total = echoes.shape[1], echoes.shape[2]
    blocks = range_total // BLOCK
    sections = (taps.shape[1] if own else taps.shape[-1] - BLOCK) // BLOCK + 1
    segments, levels, inner = planes
    bins = range_total // (CORES * segments * levels * inner)
    width = blocks // (CORES * segments)
    span = width + sections + 1
    flops = 2 * 3 * 3 * segments * (width + 2) * lines * sections * BLOCK * BLOCK
    vmem, hbm = pl.BlockSpec(memory_space=pltpu.VMEM), pl.BlockSpec(memory_space=pltpu.HBM)
    scratch = [
        pltpu.VMEM((3, 2, segments * span * lines, BLOCK), jnp.bfloat16),
        pltpu.VMEM((3, 2, segments * span * lines, BLOCK), jnp.bfloat16),
        pltpu.VMEM((2, segments * (width + 2) * lines, BLOCK), jnp.float32),
    ]
    operands = [shift_bins, taps, weights, echoes]
    if own:
        operands = [pltpu.with_memory_space_constraint(array, pltpu.HBM) for array in operands]
        in_specs = [pl.BlockSpec(memory_space=pltpu.SMEM), hbm, hbm, hbm]
        out_shape = [jax.ShapeDtypeStruct((segments, inner, 2 * lines, bins), jnp.float32)] * levels
        out_shape += [jax.ShapeDtypeStruct((3, 2, BLOCK, sections * BLOCK), jnp.bfloat16)]
        out_specs = [vmem] * (levels + 1)
        scratch = [
            pltpu.VMEM(taps.shape, jnp.float32),
            pltpu.VMEM(weights.shape, jnp.float32),
            pltpu.VMEM(echoes.shape, jnp.float32),
            *scratch,
            pltpu.SemaphoreType.DMA((3,)),
        ]
    else:
        in_specs = [pl.BlockSpec(memory_space=pltpu.SMEM), vmem, vmem, vmem]
        out_shape = jax.ShapeDtypeStruct((segments * levels * inner, 2 * lines, bins), jnp.float32)
        out_specs = hbm
        scratch += [
            pltpu.VMEM((levels, segments, inner, 2 * lines, bins), jnp.float32),
            pltpu.SemaphoreType.DMA((levels, segments)),
        ]
    return pl.pallas_call(
        functools.partial(range_kernel, own, planes, lines, blocks, sections),
        out_shape=out_shape,
        in_specs=in_specs,
        out_specs=out_specs,
        scratch_shapes=scratch,
        compiler_params=pltpu.CompilerParams(vmem_limit_bytes=24 << 20),
        cost_estimate=pl.CostEstimate(flops=flops, bytes_accessed=3 * echoes.size * 2, transcendentals=0),
        name="range_own" if own else "range_partner",
    )(*operands)


def regroup_kernel(levels, plane, *refs):
    sources, outs, sems = refs[:levels], refs[levels:-1], refs[-1]
    inner = sources[0].shape[1]
    mine = place_here(inner)
    copies = []
    for q in range(plane):
        place = mine ^ q
        for k in range(levels):
            source = sources[k].at[place // inner, lax.rem(place, inner)]
            copies.append(pltpu.make_async_copy(source, outs[q].at[k], sems.at[q, k]))
            copies[-1].start()
    for copy in copies:
        copy.wait()


def place_here(inner):
    return (lax.axis_index("gx") // CORES) * inner + lax.rem(lax.axis_index("gy"), inner)


def regroup_call(received):
    levels = len(received)
    segments, inner, rows, bins = received[0].shape
    plane = segments * inner
    return pl.pallas_call(
        functools.partial(regroup_kernel, levels, plane),
        out_shape=[jax.ShapeDtypeStruct((levels, rows, bins), jnp.float32)] * plane,
        in_specs=[pl.BlockSpec(memory_space=pl.ANY)] * levels,
        out_specs=[pl.BlockSpec(memory_space=pltpu.HBM)] * plane,
        scratch_shapes=[pltpu.SemaphoreType.DMA((plane, levels))],
        compiler_params=pltpu.CompilerParams(vmem_limit_bytes=8 << 20),
        cost_estimate=pl.CostEstimate(flops=0, bytes_accessed=8 * levels * plane * rows * bins, transcendentals=0),
        name="regroup",
    )(*received)


def azimuth_tables(taps_ref, table):
    length = taps_ref.shape[1]
    diagonals = table.shape[2]
    first = (length // BLOCK + 1 - diagonals) // 2
    zeros = jnp.zeros((1, BLOCK), jnp.float32)
    for part in range(2):
        row = jnp.concatenate([zeros, taps_ref[part : part + 1, :], zeros], axis=1)
        width = (diagonals + 1) * BLOCK
        full = toeplitz(row[:, first * BLOCK : first * BLOCK + width], BLOCK, width)
        for n in range(diagonals):
            at = (n + 1) * BLOCK
            table[part, 0, n], table[part, 1, n] = split(full[:, at : at + BLOCK])


def azimuth_sums(table, lines_ref):
    diagonals = table.shape[2]
    middle = diagonals // 2
    blocks = lines_ref.shape[1] // BLOCK
    pieces = [
        [split(lines_ref[part, b * BLOCK : (b + 1) * BLOCK, :]) for b in range(blocks)] for part in range(2)
    ]

    def product(b, taps, part):
        sums = None
        for diagonal in range(diagonals):
            other = b + diagonal - middle
            if not 0 <= other < blocks:
                continue
            m_high, m_low = pieces[part][other]
            t_high, t_low = table[taps, 0, diagonal], table[taps, 1, diagonal]
            for left, right in ((t_high, m_high), (t_high, m_low), (t_low, m_high)):
                term = lax.dot_general(left, right, PLAIN, preferred_element_type=jnp.float32)
                sums = term if sums is None else sums + term
        return sums

    for b in range(blocks):
        at = slice(b * BLOCK, (b + 1) * BLOCK)
        yield 0, at, product(b, 0, 0) + product(b, 1, 1)
        yield 1, at, product(b, 0, 1) - product(b, 1, 0)


def azimuth_kernel(planes, *refs):
    segments, levels, inner = planes
    table, moved_ref, *arrived, out_hbm, lines_ref, image, sems = refs
    lines = moved_ref.shape[1] // 2
    run = levels * inner
    core = lax.rem(lax.axis_index("gx"), CORES)
    level = lax.axis_index("gy") // inner
    mine = place_here(inner)
    for q, source in enumerate(arrived):
        place = mine ^ q
        for k in range(levels):
            device = (((place // inner) * CORES + core) * levels + (level ^ k)) * inner + lax.rem(place, inner)
            rows = pl.ds(pl.multiple_of(device * lines, lines), lines)
            for part in range(2):
                lines_ref[part, rows, :] = source[k, part * lines : (part + 1) * lines, :]
    for segment in range(segments):
        first = (CORES * segment + 1 - core) * run * lines
        rows = pl.ds(pl.multiple_of(first, run * lines), run * lines)
        for part in range(2):
            values = moved_ref[segment * run : (segment + 1) * run, part * lines : (part + 1) * lines, :]
            lines_ref[part, rows, :] = values.reshape(run * lines, values.shape[-1])
    sends = []
    for part, at, sums in azimuth_sums(table, lines_ref):
        image[part, at, :] = sums
        sends.append(pltpu.make_async_copy(image.at[part, at], out_hbm.at[part, at], sems.at[len(sends)]))
        sends[-1].start()
    for send in sends:
        send.wait()


def azimuth_call(planes, count, table, moved, arrived):
    bins = moved.shape[-1]
    vmem = pl.BlockSpec(memory_space=pltpu.VMEM)
    return pl.pallas_call(
        functools.partial(azimuth_kernel, planes),
        out_shape=jax.ShapeDtypeStruct((2, count, bins), jnp.float32),
        in_specs=[vmem] * (2 + len(arrived)),
        out_specs=pl.BlockSpec(memory_space=pltpu.HBM),
        scratch_shapes=[
            pltpu.VMEM((2, count, bins), jnp.float32),
            pltpu.VMEM((2, count, bins), jnp.float32),
            pltpu.SemaphoreType.DMA((2 * count // BLOCK,)),
        ],
        compiler_params=pltpu.CompilerParams(vmem_limit_bytes=24 << 20),
        cost_estimate=pl.CostEstimate(
            flops=2 * 3 * 4 * count * BLOCK * bins, bytes_accessed=4 * 4 * count * bins, transcendentals=0
        ),
        name="azimuth",
    )(table, moved, *arrived)


def table_call(azimuth_ref, count):
    diagonals = min(azimuth_ref.shape[1] // BLOCK + 1, 2 * (count // BLOCK) - 1)
    vmem = pl.BlockSpec(memory_space=pltpu.VMEM)
    return pl.pallas_call(
        azimuth_tables,
        out_shape=jax.ShapeDtypeStruct((2, 2, diagonals, BLOCK, BLOCK), jnp.bfloat16),
        in_specs=[vmem],
        out_specs=vmem,
        compiler_params=pltpu.CompilerParams(vmem_limit_bytes=24 << 20),
        cost_estimate=pl.CostEstimate(flops=AHEAD << 20, bytes_accessed=0, transcendentals=0),
        name="azimuth_table",
    )(azimuth_ref)


def pairs_of(planes, level_step=0, place_step=0, core_step=0):
    segments, levels, inner = planes
    pairs = []
    for device in range(CORES * segments * levels * inner):
        core = (device // (levels * inner)) % CORES
        place = (device // (CORES * levels * inner)) * inner + device % inner
        level = (device // inner) % levels
        place, level, core = place ^ place_step, level ^ level_step, core ^ core_step
        pairs.append((device, (((place // inner) * CORES + core) * levels + level) * inner + place % inner))
    return pairs


def per_device(echoes, range_ref, azimuth_ref, shift_bins, interp_weights):
    outer, run = lax.axis_size("gx"), lax.axis_size("gy")
    segments, levels = outer // CORES, LEVELS
    planes = (segments, levels, run // levels)
    devices_all = outer * run
    bins = echoes.shape[2] // devices_all
    partner = [
        lax.ppermute(array, AXES, pairs_of(planes, core_step=1)) for array in (echoes, shift_bins, interp_weights)
    ]
    *by_level, table = range_call(True, echoes, range_ref, shift_bins, interp_weights, planes)
    received = [by_level[0]] + [
        lax.ppermute(by_level[k], AXES, pairs_of(planes, level_step=k)) for k in range(1, levels)
    ]
    migrated = range_call(False, partner[0], table, partner[1], partner[2], planes)
    groups = [
        [(segment * CORES + core) * run + at for segment in range(segments) for at in range(run)]
        for core in range(CORES)
    ]
    moved = lax.all_to_all(migrated, AXES, split_axis=0, concat_axis=0, axis_index_groups=groups, tiled=True)
    *received, migrated = lax.optimization_barrier((*received, migrated))
    by_place = regroup_call(received)
    *by_place, taps_later = lax.optimization_barrier((*by_place, azimuth_ref))
    arrived = [by_place[0]] + [
        lax.ppermute(by_place[q], AXES, pairs_of(planes, place_step=q)) for q in range(1, len(by_place))
    ]
    count = devices_all * echoes.shape[1]
    return azimuth_call(planes, count, table_call(taps_later, count), moved, arrived)


def solution(mesh):
    placed = (P(None, AXES, None), P(), P(), P(AXES), P(AXES, None))
    return jax.shard_map(
        per_device,
        mesh=mesh,
        in_specs=placed,
        out_specs=P(None, None, AXES),
        check_vma=False,
    )
```

```python
import functools

import jax
import jax.numpy as jnp
from jax import lax
from jax.experimental import pallas as pl
from jax.experimental.pallas import tpu as pltpu
from jax.sharding import PartitionSpec as P

TAPS = 8
BLOCK = 256
LANE = 128
AXES = ("gx", "gy")
CORES = 2
DISTANCES = (0, 2, 3, 1)
AHEAD = 20000

ROWS_BY_ROWS = (((1,), (1,)), ((), ()))
PLAIN = (((1,), (0,)), ((), ()))


def split(values):
    high = values.astype(jnp.bfloat16)
    return high, (values - high.astype(jnp.float32)).astype(jnp.bfloat16)


def toeplitz(row, rows, width):
    if width > row.shape[1]:
        row = jnp.concatenate([row, jnp.zeros((1, width - row.shape[1]), jnp.float32)], axis=1)
    return pltpu.roll(jnp.broadcast_to(row, (rows, width)), 0, axis=1, stride=1, stride_axis=0)


def range_kernel(own, planes, lines, blocks, sections, *refs):
    if own:
        shift_ref, taps_hbm, weights_hbm, echoes_hbm, *outs, settings, table, taps_ref, weights_ref, echoes_ref, even, odd, compressed, sems = refs
    else:
        settings, table, echoes_ref, out_ref, even, odd, compressed, ready, sems = refs
    segments, levels, inner = planes
    core = lax.rem(lax.axis_index("gx"), CORES)
    width = blocks // (CORES * segments)
    halo = (sections - 1) // 2
    span = width + 2 + 2 * halo
    at_start, at_end = core == 0, core == CORES - 1
    if own:
        copies = [
            pltpu.make_async_copy(taps_hbm, taps_ref, sems.at[0]),
            pltpu.make_async_copy(weights_hbm, weights_ref, sems.at[1]),
            pltpu.make_async_copy(echoes_hbm, echoes_ref, sems.at[2]),
        ]
        for copy in copies:
            copy.start()
        copies[0].wait()
        copies[1].wait()
        real = toeplitz(taps_ref[0:1, :], BLOCK, sections * BLOCK)
        imag = toeplitz(taps_ref[1:2, :], BLOCK, sections * BLOCK)
        for kind, values in enumerate((real, imag, real - imag)):
            table[kind, 0], table[kind, 1] = split(values)
        settings[...] = settings_of(lines, shift_ref, weights_ref)
        copies[2].wait()

    def piece(segment, part, block):
        at = (CORES * segment + core) * width + block - halo - 1
        low = segment == 0 and block <= halo
        high = segment == segments - 1 and block > halo + width
        if low:
            at = jnp.maximum(at, 0)
        if high:
            at = jnp.minimum(at, blocks - 1)
        values = echoes_ref[part, :, pl.ds(pl.multiple_of(at * BLOCK, BLOCK), BLOCK)]
        if low:
            values = jnp.where(at_start, 0.0, values)
        if high:
            values = jnp.where(at_end, 0.0, values)
        return values

    for segment in range(segments):
        for offset, ref in ((0, even), (1, odd)):
            for pair in range((span - offset) // 2):
                first = 2 * pair + offset
                parts = [
                    jnp.concatenate([piece(segment, part, first), piece(segment, part, first + 1)], axis=0)
                    for part in range(2)
                ]
                at = slice((segment * span + 2 * pair) * lines, (segment * span + 2 * pair + 2) * lines)
                for kind, values in enumerate((parts[0], parts[1], parts[0] + parts[1])):
                    ref[kind, 0, at, :], ref[kind, 1, at, :] = split(values)
    rows = (width + 2) * lines
    products = []
    for kind in range(3):
        sums = None
        for section in range(sections):
            ref = even if section % 2 == 0 else odd
            starts = [(segment * span + section - section % 2) * lines for segment in range(segments)]
            x_high, x_low = [
                jnp.concatenate([ref[kind, which, start : start + rows, :] for start in starts], axis=0)
                for which in range(2)
            ]
            at = slice(section * BLOCK, (section + 1) * BLOCK)
            t_high, t_low = table[kind, 0, :, at], table[kind, 1, :, at]
            for left, right in ((x_high, t_high), (x_low, t_high), (x_high, t_low)):
                term = lax.dot_general(left, right, ROWS_BY_ROWS, preferred_element_type=jnp.float32)
                sums = term if sums is None else sums + term
        products.append(sums)
    compressed[0] = products[0] + products[1]
    compressed[1] = products[2] - products[0] + products[1]
    for part in range(2):
        low, high = slice(0, lines), slice(segments * rows - lines, segments * rows)
        compressed[part, low, :] = jnp.where(at_start, 0.0, compressed[part, low, :])
        compressed[part, high, :] = jnp.where(at_end, 0.0, compressed[part, high, :])

    plan = migration_plan(settings[...])
    sends = []
    run = width // levels
    for step in range(levels):
        level = (lax.axis_index("gy") // inner) ^ DISTANCES[step] if own else step
        streams = [(segment, part) for segment in range(segments) for part in range(2)]

        def loader(segment, part):
            first = (segment * (width + 2) + 1 + level * run) * lines

            def load(tile):
                block, at = tile * LANE // BLOCK, tile * LANE % BLOCK
                start = first + block * lines
                if own:
                    start = pl.multiple_of(start, lines)
                return compressed[part, pl.ds(start, lines), at : at + LANE]

            return load

        moved = migrate(run * BLOCK // LANE, plan, [loader(*stream) for stream in streams])
        for (segment, part), row in zip(streams, moved):
            target = (outs[step] if own else ready.at[step]).at[segment]
            per = target.shape[-1] // LANE
            for tile, values in enumerate(row):
                at = (tile % per) * LANE
                target[tile // per, part * lines : (part + 1) * lines, at : at + LANE] = values
        if not own:
            for segment in range(segments):
                first = (segment * levels + step) * inner
                sends.append(
                    pltpu.make_async_copy(
                        ready.at[step, segment], out_ref.at[first : first + inner], sems.at[step, segment]
                    )
                )
                sends[-1].start()
    for send in sends:
        send.wait()


def settings_of(lines, shift_ref, weights_ref):
    lane = lax.broadcasted_iota(jnp.int32, (lines, LANE), 1)
    row = lax.broadcasted_iota(jnp.int32, (lines, LANE), 0)
    settings = jnp.zeros((lines, LANE), jnp.float32)
    for line in range(lines):
        settings = jnp.where((row == line) & (lane == TAPS), shift_ref[line].astype(jnp.float32), settings)
    for j in range(TAPS):
        settings = jnp.where(lane == j, weights_ref[:, j : j + 1], settings)
    return settings


def migration_plan(settings):
    lines = settings.shape[0]
    lane = lax.broadcasted_iota(jnp.int32, (lines, LANE), 1)
    columns = [jnp.broadcast_to(settings[:, j : j + 1], (lines, LANE)) for j in range(TAPS + 1)]
    shift = columns[TAPS].astype(jnp.int32)
    steps = []
    for step in range(2):
        place = lane + shift - (TAPS // 2 - 1) + step
        steps.append((place & (LANE - 1), place < 0, place >= LANE))
    return steps, columns[:TAPS], lane


def migrate(tiles, plan, loads):
    steps, weights, lane = plan
    pairs = []
    for index, below, above in steps:
        turned = [
            [
                jnp.take_along_axis(load(tile), index, axis=1, mode="promise_in_bounds")
                for tile in range(-1, tiles + 2)
            ]
            for load in loads
        ]
        pairs.append(
            [
                [
                    jnp.where(below, row[tile], jnp.where(above, row[tile + 2], row[tile + 1]))
                    for tile in range(tiles + 1)
                ]
                for row in turned
            ]
        )
    totals = None
    for k in range(TAPS // 2):
        terms = [
            [weights[2 * k] * one + weights[2 * k + 1] * two for one, two in zip(*rows)] for rows in zip(*pairs)
        ]
        if k == 0:
            totals = [row[:tiles] for row in terms]
            continue
        rolled = [[pltpu.roll(term, LANE - 2 * k, axis=1) for term in row] for row in terms]
        inside = lane < LANE - 2 * k
        totals = [
            [total[tile] + jnp.where(inside, row[tile], row[tile + 1]) for tile in range(tiles)]
            for total, row in zip(totals, rolled)
        ]
    return totals


def range_call(own, planes, echoes, taps, *settings):
    lines, range_total = echoes.shape[1], echoes.shape[2]
    blocks = range_total // BLOCK
    sections = (taps.shape[1] if own else taps.shape[-1] - BLOCK) // BLOCK + 1
    segments, levels, inner = planes
    bins = range_total // (CORES * segments * levels * inner)
    width = blocks // (CORES * segments)
    span = width + sections + 1
    flops = 2 * 3 * 3 * segments * (width + 2) * lines * sections * BLOCK * BLOCK
    vmem, hbm = pl.BlockSpec(memory_space=pltpu.VMEM), pl.BlockSpec(memory_space=pltpu.HBM)
    scratch = [
        pltpu.VMEM((3, 2, segments * span * lines, BLOCK), jnp.bfloat16),
        pltpu.VMEM((3, 2, segments * span * lines, BLOCK), jnp.bfloat16),
        pltpu.VMEM((2, segments * (width + 2) * lines, BLOCK), jnp.float32),
    ]
    if own:
        shift_bins, weights = settings
        operands = [shift_bins, taps, weights, echoes]
        operands = [pltpu.with_memory_space_constraint(array, pltpu.HBM) for array in operands]
        in_specs = [pl.BlockSpec(memory_space=pltpu.SMEM), hbm, hbm, hbm]
        out_shape = [jax.ShapeDtypeStruct((segments, inner, 2 * lines, bins), jnp.float32)] * levels
        out_shape += [jax.ShapeDtypeStruct((lines, LANE), jnp.float32)]
        out_shape += [jax.ShapeDtypeStruct((3, 2, BLOCK, sections * BLOCK), jnp.bfloat16)]
        out_specs = [vmem] * (levels + 2)
        scratch = [
            pltpu.VMEM(taps.shape, jnp.float32),
            pltpu.VMEM(weights.shape, jnp.float32),
            pltpu.VMEM(echoes.shape, jnp.float32),
            *scratch,
            pltpu.SemaphoreType.DMA((3,)),
        ]
    else:
        operands = [*settings, taps, echoes]
        in_specs = [vmem] * 3
        out_shape = jax.ShapeDtypeStruct((segments * levels * inner, 2 * lines, bins), jnp.float32)
        out_specs = hbm
        scratch += [
            pltpu.VMEM((levels, segments, inner, 2 * lines, bins), jnp.float32),
            pltpu.SemaphoreType.DMA((levels, segments)),
        ]
    return pl.pallas_call(
        functools.partial(range_kernel, own, planes, lines, blocks, sections),
        out_shape=out_shape,
        in_specs=in_specs,
        out_specs=out_specs,
        scratch_shapes=scratch,
        compiler_params=pltpu.CompilerParams(vmem_limit_bytes=24 << 20),
        cost_estimate=pl.CostEstimate(flops=flops, bytes_accessed=3 * echoes.size * 2, transcendentals=0),
        name="range_own" if own else "range_partner",
    )(*operands)


def regroup_kernel(levels, plane, *refs):
    sources, outs, sems = refs[:levels], refs[levels:-1], refs[-1]
    inner = sources[0].shape[1]
    mine = place_here(inner)
    copies = []
    for q in range(plane):
        place = mine ^ q
        for k in range(levels):
            source = sources[k].at[place // inner, lax.rem(place, inner)]
            copies.append(pltpu.make_async_copy(source, outs[q].at[k], sems.at[q, k]))
            copies[-1].start()
    for copy in copies:
        copy.wait()


def place_here(inner):
    return (lax.axis_index("gx") // CORES) * inner + lax.rem(lax.axis_index("gy"), inner)


def regroup_call(received):
    levels = len(received)
    segments, inner, rows, bins = received[0].shape
    plane = segments * inner
    return pl.pallas_call(
        functools.partial(regroup_kernel, levels, plane),
        out_shape=[jax.ShapeDtypeStruct((levels, rows, bins), jnp.float32)] * plane,
        in_specs=[pl.BlockSpec(memory_space=pl.ANY)] * levels,
        out_specs=[pl.BlockSpec(memory_space=pltpu.HBM)] * plane,
        scratch_shapes=[pltpu.SemaphoreType.DMA((plane, levels))],
        compiler_params=pltpu.CompilerParams(vmem_limit_bytes=8 << 20),
        cost_estimate=pl.CostEstimate(flops=0, bytes_accessed=8 * levels * plane * rows * bins, transcendentals=0),
        name="regroup",
    )(*received)


def azimuth_tables(taps_ref, table):
    length = taps_ref.shape[1]
    diagonals = table.shape[2]
    first = (length // BLOCK + 1 - diagonals) // 2
    zeros = jnp.zeros((1, BLOCK), jnp.float32)
    for part in range(2):
        row = jnp.concatenate([zeros, taps_ref[part : part + 1, :], zeros], axis=1)
        width = (diagonals + 1) * BLOCK
        full = toeplitz(row[:, first * BLOCK : first * BLOCK + width], BLOCK, width)
        for n in range(diagonals):
            at = (n + 1) * BLOCK
            table[part, 0, n], table[part, 1, n] = split(full[:, at : at + BLOCK])


def azimuth_sums(table, lines_ref):
    diagonals = table.shape[2]
    middle = diagonals // 2
    blocks = lines_ref.shape[1] // BLOCK
    pieces = [
        [split(lines_ref[part, b * BLOCK : (b + 1) * BLOCK, :]) for b in range(blocks)] for part in range(2)
    ]

    def product(b, taps, part):
        sums = None
        for diagonal in range(diagonals):
            other = b + diagonal - middle
            if not 0 <= other < blocks:
                continue
            m_high, m_low = pieces[part][other]
            t_high, t_low = table[taps, 0, diagonal], table[taps, 1, diagonal]
            for left, right in ((t_high, m_high), (t_high, m_low), (t_low, m_high)):
                term = lax.dot_general(left, right, PLAIN, preferred_element_type=jnp.float32)
                sums = term if sums is None else sums + term
        return sums

    for b in range(blocks):
        at = slice(b * BLOCK, (b + 1) * BLOCK)
        yield 0, at, product(b, 0, 0) + product(b, 1, 1)
        yield 1, at, product(b, 0, 1) - product(b, 1, 0)


def azimuth_kernel(planes, *refs):
    segments, levels, inner = planes
    table, moved_ref, *arrived, out_hbm, lines_ref, image, sems = refs
    lines = moved_ref.shape[1] // 2
    run = levels * inner
    core = lax.rem(lax.axis_index("gx"), CORES)
    level = lax.axis_index("gy") // inner
    mine = place_here(inner)
    for q, source in enumerate(arrived):
        place = mine ^ q
        for k in range(levels):
            device = (((place // inner) * CORES + core) * levels + (level ^ DISTANCES[k])) * inner + lax.rem(place, inner)
            rows = pl.ds(pl.multiple_of(device * lines, lines), lines)
            for part in range(2):
                lines_ref[part, rows, :] = source[k, part * lines : (part + 1) * lines, :]
    for segment in range(segments):
        first = (CORES * segment + 1 - core) * run * lines
        rows = pl.ds(pl.multiple_of(first, run * lines), run * lines)
        for part in range(2):
            values = moved_ref[segment * run : (segment + 1) * run, part * lines : (part + 1) * lines, :]
            lines_ref[part, rows, :] = values.reshape(run * lines, values.shape[-1])
    sends = []
    for part, at, sums in azimuth_sums(table, lines_ref):
        image[part, at, :] = sums
        sends.append(pltpu.make_async_copy(image.at[part, at], out_hbm.at[part, at], sems.at[len(sends)]))
        sends[-1].start()
    for send in sends:
        send.wait()


def azimuth_call(planes, count, table, moved, arrived):
    bins = moved.shape[-1]
    vmem = pl.BlockSpec(memory_space=pltpu.VMEM)
    return pl.pallas_call(
        functools.partial(azimuth_kernel, planes),
        out_shape=jax.ShapeDtypeStruct((2, count, bins), jnp.float32),
        in_specs=[vmem] * (2 + len(arrived)),
        out_specs=pl.BlockSpec(memory_space=pltpu.HBM),
        scratch_shapes=[
            pltpu.VMEM((2, count, bins), jnp.float32),
            pltpu.VMEM((2, count, bins), jnp.float32),
            pltpu.SemaphoreType.DMA((2 * count // BLOCK,)),
        ],
        compiler_params=pltpu.CompilerParams(vmem_limit_bytes=24 << 20),
        cost_estimate=pl.CostEstimate(
            flops=2 * 3 * 4 * count * BLOCK * bins, bytes_accessed=4 * 4 * count * bins, transcendentals=0
        ),
        name="azimuth",
    )(table, moved, *arrived)


def table_call(azimuth_ref, count):
    diagonals = min(azimuth_ref.shape[1] // BLOCK + 1, 2 * (count // BLOCK) - 1)
    vmem = pl.BlockSpec(memory_space=pltpu.VMEM)
    return pl.pallas_call(
        azimuth_tables,
        out_shape=jax.ShapeDtypeStruct((2, 2, diagonals, BLOCK, BLOCK), jnp.bfloat16),
        in_specs=[vmem],
        out_specs=vmem,
        compiler_params=pltpu.CompilerParams(vmem_limit_bytes=24 << 20),
        cost_estimate=pl.CostEstimate(flops=AHEAD << 20, bytes_accessed=0, transcendentals=0),
        name="azimuth_table",
    )(azimuth_ref)


def pairs_of(planes, level_step=0, place_step=0, core_step=0):
    segments, levels, inner = planes
    pairs = []
    for device in range(CORES * segments * levels * inner):
        core = (device // (levels * inner)) % CORES
        place = (device // (CORES * levels * inner)) * inner + device % inner
        level = (device // inner) % levels
        place, level, core = place ^ place_step, level ^ level_step, core ^ core_step
        pairs.append((device, (((place // inner) * CORES + core) * levels + level) * inner + place % inner))
    return pairs


def per_device(echoes, range_ref, azimuth_ref, shift_bins, interp_weights):
    outer, run = lax.axis_size("gx"), lax.axis_size("gy")
    segments, levels = outer // CORES, len(DISTANCES)
    planes = (segments, levels, run // levels)
    devices_all = outer * run
    bins = echoes.shape[2] // devices_all
    echoes_partner = lax.ppermute(echoes, AXES, pairs_of(planes, core_step=1))
    *by_level, settings, table = range_call(True, planes, echoes, range_ref, shift_bins, interp_weights)
    received = [by_level[0]] + [
        lax.ppermute(array, AXES, pairs_of(planes, level_step=distance))
        for distance, array in zip(DISTANCES[1:], by_level[1:])
    ]
    settings_partner = lax.ppermute(settings, AXES, pairs_of(planes, core_step=1))
    migrated = range_call(False, planes, echoes_partner, table, settings_partner)
    groups = [
        [(segment * CORES + core) * run + at for segment in range(segments) for at in range(run)]
        for core in range(CORES)
    ]
    moved = lax.all_to_all(migrated, AXES, split_axis=0, concat_axis=0, axis_index_groups=groups, tiled=True)
    *received, migrated = lax.optimization_barrier((*received, migrated))
    by_place = regroup_call(received)
    *by_place, taps_later = lax.optimization_barrier((*by_place, azimuth_ref))
    arrived = [by_place[0]] + [
        lax.ppermute(by_place[q], AXES, pairs_of(planes, place_step=q)) for q in range(1, len(by_place))
    ]
    count = devices_all * echoes.shape[1]
    return azimuth_call(planes, count, table_call(taps_later, count), moved, arrived)


def solution(mesh):
    placed = (P(None, AXES, None), P(), P(), P(AXES), P(AXES, None))
    return jax.shard_map(
        per_device,
        mesh=mesh,
        in_specs=placed,
        out_specs=P(None, None, AXES),
        check_vma=False,
    )
```

```python
import functools

import jax
import jax.numpy as jnp
from jax import lax
from jax.experimental import pallas as pl
from jax.experimental.pallas import tpu as pltpu
from jax.sharding import PartitionSpec as P

TAPS = 8
BLOCK = 256
LANE = 128
AXES = ("gx", "gy")
CORES = 2
DISTANCES = (0, 2, 3, 1)
AHEAD = 20000

ROWS_BY_ROWS = (((1,), (1,)), ((), ()))
PLAIN = (((1,), (0,)), ((), ()))


def split(values):
    high = values.astype(jnp.bfloat16)
    return high, (values - high.astype(jnp.float32)).astype(jnp.bfloat16)


def toeplitz(row, rows, width):
    if width > row.shape[1]:
        row = jnp.concatenate([row, jnp.zeros((1, width - row.shape[1]), jnp.float32)], axis=1)
    return pltpu.roll(jnp.broadcast_to(row, (rows, width)), 0, axis=1, stride=1, stride_axis=0)


def range_kernel(own, planes, lines, blocks, sections, *refs):
    if own:
        shift_ref, taps_hbm, weights_hbm, echoes_hbm, *outs, settings, table, taps_ref, weights_ref, echoes_ref, even, odd, compressed, sems = refs
    else:
        settings, table, echoes_ref, out_ref, even, odd, compressed, ready, sems = refs
    segments, levels, inner = planes
    core = lax.rem(lax.axis_index("gx"), CORES)
    width = blocks // (CORES * segments)
    halo = (sections - 1) // 2
    span = width + 2 + 2 * halo
    at_start, at_end = core == 0, core == CORES - 1
    if own:
        copies = [
            pltpu.make_async_copy(taps_hbm, taps_ref, sems.at[0]),
            pltpu.make_async_copy(weights_hbm, weights_ref, sems.at[1]),
            pltpu.make_async_copy(echoes_hbm, echoes_ref, sems.at[2]),
        ]
        for copy in copies:
            copy.start()
        copies[0].wait()
        copies[1].wait()
        real = toeplitz(taps_ref[0:1, :], BLOCK, sections * BLOCK)
        imag = toeplitz(taps_ref[1:2, :], BLOCK, sections * BLOCK)
        for kind, values in enumerate((real, imag, real - imag)):
            table[kind, 0], table[kind, 1] = split(values)
        settings[...] = settings_of(lines, shift_ref, weights_ref)
        copies[2].wait()

    def piece(segment, part, block):
        at = (CORES * segment + core) * width + block - halo - 1
        low = segment == 0 and block <= halo
        high = segment == segments - 1 and block > halo + width
        if low:
            at = jnp.maximum(at, 0)
        if high:
            at = jnp.minimum(at, blocks - 1)
        values = echoes_ref[part, :, pl.ds(pl.multiple_of(at * BLOCK, BLOCK), BLOCK)]
        if low:
            values = jnp.where(at_start, 0.0, values)
        if high:
            values = jnp.where(at_end, 0.0, values)
        return values

    for segment in range(segments):
        for offset, ref in ((0, even), (1, odd)):
            for pair in range((span - offset) // 2):
                first = 2 * pair + offset
                parts = [
                    jnp.concatenate([piece(segment, part, first), piece(segment, part, first + 1)], axis=0)
                    for part in range(2)
                ]
                at = slice((segment * span + 2 * pair) * lines, (segment * span + 2 * pair + 2) * lines)
                for kind, values in enumerate((parts[0], parts[1], parts[0] + parts[1])):
                    ref[kind, 0, at, :], ref[kind, 1, at, :] = split(values)
    rows = (width + 2) * lines
    products = []
    for kind in range(3):
        sums = None
        for section in range(sections):
            ref = even if section % 2 == 0 else odd
            starts = [(segment * span + section - section % 2) * lines for segment in range(segments)]
            x_high, x_low = [
                jnp.concatenate([ref[kind, which, start : start + rows, :] for start in starts], axis=0)
                for which in range(2)
            ]
            at = slice(section * BLOCK, (section + 1) * BLOCK)
            t_high, t_low = table[kind, 0, :, at], table[kind, 1, :, at]
            for left, right in ((x_high, t_high), (x_low, t_high), (x_high, t_low)):
                term = lax.dot_general(left, right, ROWS_BY_ROWS, preferred_element_type=jnp.float32)
                sums = term if sums is None else sums + term
        products.append(sums)
    compressed[0] = products[0] + products[1]
    compressed[1] = products[2] - products[0] + products[1]
    for part in range(2):
        low, high = slice(0, lines), slice(segments * rows - lines, segments * rows)
        compressed[part, low, :] = jnp.where(at_start, 0.0, compressed[part, low, :])
        compressed[part, high, :] = jnp.where(at_end, 0.0, compressed[part, high, :])

    plan = migration_plan(settings[...])
    sends = []
    run = width // levels
    for step in range(levels):
        level = (lax.axis_index("gy") // inner) ^ DISTANCES[step] if own else step
        streams = [(segment, part) for segment in range(segments) for part in range(2)]

        def loader(segment, part):
            first = (segment * (width + 2) + 1 + level * run) * lines

            def load(tile):
                block, at = tile * LANE // BLOCK, tile * LANE % BLOCK
                start = first + block * lines
                if own:
                    start = pl.multiple_of(start, lines)
                return compressed[part, pl.ds(start, lines), at : at + LANE]

            return load

        moved = migrate(run * BLOCK // LANE, plan, [loader(*stream) for stream in streams])
        for (segment, part), row in zip(streams, moved):
            target = (outs[step] if own else ready.at[step]).at[segment]
            per = target.shape[-1] // LANE
            for tile, values in enumerate(row):
                at = (tile % per) * LANE
                target[tile // per, part * lines : (part + 1) * lines, at : at + LANE] = values
        if not own:
            for segment in range(segments):
                first = (segment * levels + step) * inner
                sends.append(
                    pltpu.make_async_copy(
                        ready.at[step, segment], out_ref.at[first : first + inner], sems.at[step, segment]
                    )
                )
                sends[-1].start()
    for send in sends:
        send.wait()


def settings_of(lines, shift_ref, weights_ref):
    lane = lax.broadcasted_iota(jnp.int32, (lines, LANE), 1)
    row = lax.broadcasted_iota(jnp.int32, (lines, LANE), 0)
    settings = jnp.zeros((lines, LANE), jnp.float32)
    for line in range(lines):
        settings = jnp.where((row == line) & (lane == TAPS), shift_ref[line].astype(jnp.float32), settings)
    for j in range(TAPS):
        settings = jnp.where(lane == j, weights_ref[:, j : j + 1], settings)
    return settings


def migration_plan(settings):
    lines = settings.shape[0]
    lane = lax.broadcasted_iota(jnp.int32, (lines, LANE), 1)
    columns = [jnp.broadcast_to(settings[:, j : j + 1], (lines, LANE)) for j in range(TAPS + 1)]
    shift = columns[TAPS].astype(jnp.int32)
    steps = []
    for step in range(2):
        place = lane + shift - (TAPS // 2 - 1) + step
        steps.append((place & (LANE - 1), place < 0, place >= LANE))
    return steps, columns[:TAPS], lane


def migrate(tiles, plan, loads):
    steps, weights, lane = plan
    pairs = []
    for index, below, above in steps:
        turned = [
            [
                jnp.take_along_axis(load(tile), index, axis=1, mode="promise_in_bounds")
                for tile in range(-1, tiles + 2)
            ]
            for load in loads
        ]
        pairs.append(
            [
                [
                    jnp.where(below, row[tile], jnp.where(above, row[tile + 2], row[tile + 1]))
                    for tile in range(tiles + 1)
                ]
                for row in turned
            ]
        )
    totals = None
    for k in range(TAPS // 2):
        terms = [
            [weights[2 * k] * one + weights[2 * k + 1] * two for one, two in zip(*rows)] for rows in zip(*pairs)
        ]
        if k == 0:
            totals = [row[:tiles] for row in terms]
            continue
        rolled = [[pltpu.roll(term, LANE - 2 * k, axis=1) for term in row] for row in terms]
        inside = lane < LANE - 2 * k
        totals = [
            [total[tile] + jnp.where(inside, row[tile], row[tile + 1]) for tile in range(tiles)]
            for total, row in zip(totals, rolled)
        ]
    return totals


def range_call(own, planes, echoes, taps, *settings):
    lines, range_total = echoes.shape[1], echoes.shape[2]
    blocks = range_total // BLOCK
    sections = (taps.shape[1] if own else taps.shape[-1] - BLOCK) // BLOCK + 1
    segments, levels, inner = planes
    bins = range_total // (CORES * segments * levels * inner)
    width = blocks // (CORES * segments)
    span = width + sections + 1
    flops = 2 * 3 * 3 * segments * (width + 2) * lines * sections * BLOCK * BLOCK
    vmem, hbm = pl.BlockSpec(memory_space=pltpu.VMEM), pl.BlockSpec(memory_space=pltpu.HBM)
    scratch = [
        pltpu.VMEM((3, 2, segments * span * lines, BLOCK), jnp.bfloat16),
        pltpu.VMEM((3, 2, segments * span * lines, BLOCK), jnp.bfloat16),
        pltpu.VMEM((2, segments * (width + 2) * lines, BLOCK), jnp.float32),
    ]
    if own:
        shift_bins, weights = settings
        operands = [shift_bins, taps, weights, echoes]
        operands = [pltpu.with_memory_space_constraint(array, pltpu.HBM) for array in operands]
        in_specs = [pl.BlockSpec(memory_space=pltpu.SMEM), hbm, hbm, hbm]
        out_shape = [jax.ShapeDtypeStruct((segments, inner, 2 * lines, bins), jnp.float32)] * levels
        out_shape += [jax.ShapeDtypeStruct((lines, LANE), jnp.float32)]
        out_shape += [jax.ShapeDtypeStruct((3, 2, BLOCK, sections * BLOCK), jnp.bfloat16)]
        out_specs = [vmem] * (levels + 2)
        scratch = [
            pltpu.VMEM(taps.shape, jnp.float32),
            pltpu.VMEM(weights.shape, jnp.float32),
            pltpu.VMEM(echoes.shape, jnp.float32),
            *scratch,
            pltpu.SemaphoreType.DMA((3,)),
        ]
    else:
        operands = [*settings, taps, echoes]
        in_specs = [vmem] * 3
        out_shape = jax.ShapeDtypeStruct((segments * levels * inner, 2 * lines, bins), jnp.float32)
        out_specs = hbm
        scratch += [
            pltpu.VMEM((levels, segments, inner, 2 * lines, bins), jnp.float32),
            pltpu.SemaphoreType.DMA((levels, segments)),
        ]
    return pl.pallas_call(
        functools.partial(range_kernel, own, planes, lines, blocks, sections),
        out_shape=out_shape,
        in_specs=in_specs,
        out_specs=out_specs,
        scratch_shapes=scratch,
        compiler_params=pltpu.CompilerParams(vmem_limit_bytes=24 << 20),
        cost_estimate=pl.CostEstimate(flops=flops, bytes_accessed=3 * echoes.size * 2, transcendentals=0),
        name="range_own" if own else "range_partner",
    )(*operands)


def regroup_kernel(levels, plane, *refs):
    sources, outs = refs[:levels], refs[levels:]
    inner = sources[0].shape[1]
    mine = place_here(inner)
    for q in range(plane):
        place = mine ^ q
        for k in range(levels):
            outs[q][k] = sources[k][place // inner, lax.rem(place, inner)]


def place_here(inner):
    return (lax.axis_index("gx") // CORES) * inner + lax.rem(lax.axis_index("gy"), inner)


def regroup_call(received):
    levels = len(received)
    segments, inner, rows, bins = received[0].shape
    plane = segments * inner
    return pl.pallas_call(
        functools.partial(regroup_kernel, levels, plane),
        out_shape=[jax.ShapeDtypeStruct((levels, rows, bins), jnp.float32)] * plane,
        in_specs=[pl.BlockSpec(memory_space=pltpu.VMEM)] * levels,
        out_specs=[pl.BlockSpec(memory_space=pltpu.VMEM)] * plane,
        compiler_params=pltpu.CompilerParams(vmem_limit_bytes=8 << 20),
        cost_estimate=pl.CostEstimate(flops=0, bytes_accessed=8 * levels * plane * rows * bins, transcendentals=0),
        name="regroup",
    )(*received)


def azimuth_tables(taps_ref, table):
    length = taps_ref.shape[1]
    diagonals = table.shape[2]
    first = (length // BLOCK + 1 - diagonals) // 2
    zeros = jnp.zeros((1, BLOCK), jnp.float32)
    width = (diagonals + 1) * BLOCK
    full = []
    for part in range(2):
        row = jnp.concatenate([zeros, taps_ref[part : part + 1, :], zeros], axis=1)
        full.append(toeplitz(row[:, first * BLOCK : first * BLOCK + width], BLOCK, width))
    for kind, values in enumerate((full[0], full[1], full[0] - full[1])):
        for n in range(diagonals):
            at = (n + 1) * BLOCK
            table[kind, 0, n], table[kind, 1, n] = split(values[:, at : at + BLOCK])


def azimuth_sums(table, lines_ref):
    diagonals = table.shape[2]
    middle = diagonals // 2
    blocks = lines_ref.shape[1] // BLOCK
    pieces = [[], [], []]
    for b in range(blocks):
        real, imag = [lines_ref[part, b * BLOCK : (b + 1) * BLOCK, :] for part in range(2)]
        for kind, values in enumerate((real, imag, real + imag)):
            pieces[kind].append(split(values))

    def product(b, kind):
        sums = None
        for diagonal in range(diagonals):
            other = b + diagonal - middle
            if not 0 <= other < blocks:
                continue
            m_high, m_low = pieces[kind][other]
            t_high, t_low = table[kind, 0, diagonal], table[kind, 1, diagonal]
            for left, right in ((t_high, m_high), (t_high, m_low), (t_low, m_high)):
                term = lax.dot_general(left, right, PLAIN, preferred_element_type=jnp.float32)
                sums = term if sums is None else sums + term
        return sums

    for b in range(blocks):
        at = slice(b * BLOCK, (b + 1) * BLOCK)
        first, second = product(b, 0), product(b, 1)
        yield 0, at, first + second
        yield 1, at, product(b, 2) - first + second


def azimuth_kernel(planes, *refs):
    segments, levels, inner = planes
    table, moved_ref, *arrived, out_hbm, lines_ref, image, sems = refs
    lines = moved_ref.shape[1] // 2
    run = levels * inner
    core = lax.rem(lax.axis_index("gx"), CORES)
    level = lax.axis_index("gy") // inner
    mine = place_here(inner)
    for q, source in enumerate(arrived):
        place = mine ^ q
        for k in range(levels):
            device = (((place // inner) * CORES + core) * levels + (level ^ DISTANCES[k])) * inner + lax.rem(place, inner)
            rows = pl.ds(pl.multiple_of(device * lines, lines), lines)
            for part in range(2):
                lines_ref[part, rows, :] = source[k, part * lines : (part + 1) * lines, :]
    for segment in range(segments):
        first = (CORES * segment + 1 - core) * run * lines
        rows = pl.ds(pl.multiple_of(first, run * lines), run * lines)
        for part in range(2):
            values = moved_ref[segment * run : (segment + 1) * run, part * lines : (part + 1) * lines, :]
            lines_ref[part, rows, :] = values.reshape(run * lines, values.shape[-1])
    sends = []
    for part, at, sums in azimuth_sums(table, lines_ref):
        image[part, at, :] = sums
        sends.append(pltpu.make_async_copy(image.at[part, at], out_hbm.at[part, at], sems.at[len(sends)]))
        sends[-1].start()
    for send in sends:
        send.wait()


def azimuth_call(planes, count, table, moved, arrived):
    bins = moved.shape[-1]
    vmem = pl.BlockSpec(memory_space=pltpu.VMEM)
    return pl.pallas_call(
        functools.partial(azimuth_kernel, planes),
        out_shape=jax.ShapeDtypeStruct((2, count, bins), jnp.float32),
        in_specs=[vmem] * (2 + len(arrived)),
        out_specs=pl.BlockSpec(memory_space=pltpu.HBM),
        scratch_shapes=[
            pltpu.VMEM((2, count, bins), jnp.float32),
            pltpu.VMEM((2, count, bins), jnp.float32),
            pltpu.SemaphoreType.DMA((2 * count // BLOCK,)),
        ],
        compiler_params=pltpu.CompilerParams(vmem_limit_bytes=24 << 20),
        cost_estimate=pl.CostEstimate(
            flops=2 * 3 * 4 * count * BLOCK * bins, bytes_accessed=4 * 4 * count * bins, transcendentals=0
        ),
        name="azimuth",
    )(table, moved, *arrived)


def table_call(azimuth_ref, count):
    diagonals = min(azimuth_ref.shape[1] // BLOCK + 1, 2 * (count // BLOCK) - 1)
    vmem = pl.BlockSpec(memory_space=pltpu.VMEM)
    return pl.pallas_call(
        azimuth_tables,
        out_shape=jax.ShapeDtypeStruct((3, 2, diagonals, BLOCK, BLOCK), jnp.bfloat16),
        in_specs=[vmem],
        out_specs=vmem,
        compiler_params=pltpu.CompilerParams(vmem_limit_bytes=24 << 20),
        cost_estimate=pl.CostEstimate(flops=AHEAD << 20, bytes_accessed=0, transcendentals=0),
        name="azimuth_table",
    )(azimuth_ref)


def pairs_of(planes, level_step=0, place_step=0, core_step=0):
    segments, levels, inner = planes
    pairs = []
    for device in range(CORES * segments * levels * inner):
        core = (device // (levels * inner)) % CORES
        place = (device // (CORES * levels * inner)) * inner + device % inner
        level = (device // inner) % levels
        place, level, core = place ^ place_step, level ^ level_step, core ^ core_step
        pairs.append((device, (((place // inner) * CORES + core) * levels + level) * inner + place % inner))
    return pairs


def per_device(echoes, range_ref, azimuth_ref, shift_bins, interp_weights):
    outer, run = lax.axis_size("gx"), lax.axis_size("gy")
    segments, levels = outer // CORES, len(DISTANCES)
    planes = (segments, levels, run // levels)
    devices_all = outer * run
    bins = echoes.shape[2] // devices_all
    echoes_partner = lax.ppermute(echoes, AXES, pairs_of(planes, core_step=1))
    *by_level, settings, table = range_call(True, planes, echoes, range_ref, shift_bins, interp_weights)
    received = [by_level[0]] + [
        lax.ppermute(array, AXES, pairs_of(planes, level_step=distance))
        for distance, array in zip(DISTANCES[1:], by_level[1:])
    ]
    settings_partner = lax.ppermute(settings, AXES, pairs_of(planes, core_step=1))
    migrated = range_call(False, planes, echoes_partner, table, settings_partner)
    groups = [
        [(segment * CORES + core) * run + at for segment in range(segments) for at in range(run)]
        for core in range(CORES)
    ]
    moved = lax.all_to_all(migrated, AXES, split_axis=0, concat_axis=0, axis_index_groups=groups, tiled=True)
    *received, migrated = lax.optimization_barrier((*received, migrated))
    by_place = regroup_call(received)
    *by_place, taps_later = lax.optimization_barrier((*by_place, azimuth_ref))
    arrived = [by_place[0]] + [
        lax.ppermute(by_place[q], AXES, pairs_of(planes, place_step=q)) for q in range(1, len(by_place))
    ]
    count = devices_all * echoes.shape[1]
    return azimuth_call(planes, count, table_call(taps_later, count), moved, arrived)


def solution(mesh):
    placed = (P(None, AXES, None), P(), P(), P(AXES), P(AXES, None))
    return jax.shard_map(
        per_device,
        mesh=mesh,
        in_specs=placed,
        out_specs=P(None, None, AXES),
        check_vma=False,
    )
```

```python
import functools

import jax
import jax.numpy as jnp
from jax import lax
from jax.experimental import pallas as pl
from jax.experimental.pallas import tpu as pltpu
from jax.sharding import PartitionSpec as P

TAPS = 8
BLOCK = 256
LANE = 128
AXES = ("gx", "gy")
CORES = 2
DISTANCES = (0, 2, 3, 1)
AHEAD = 20000

ROWS_BY_ROWS = (((1,), (1,)), ((), ()))
PLAIN = (((1,), (0,)), ((), ()))


def split(values):
    high = values.astype(jnp.bfloat16)
    return high, (values - high.astype(jnp.float32)).astype(jnp.bfloat16)


def toeplitz(row, rows, width):
    if width > row.shape[1]:
        row = jnp.concatenate([row, jnp.zeros((1, width - row.shape[1]), jnp.float32)], axis=1)
    return pltpu.roll(jnp.broadcast_to(row, (rows, width)), 0, axis=1, stride=1, stride_axis=0)


def range_kernel(own, planes, lines, blocks, sections, *refs):
    if own:
        shift_ref, taps_hbm, weights_hbm, echoes_hbm, *outs, settings, table, taps_ref, weights_ref, echoes_ref, even, odd, compressed, sems = refs
    else:
        settings, table, echoes_ref, out_ref, even, odd, compressed, ready, sems = refs
    segments, levels, inner = planes
    core = lax.rem(lax.axis_index("gx"), CORES)
    width = blocks // (CORES * segments)
    halo = (sections - 1) // 2
    span = width + 2 + 2 * halo
    at_start, at_end = core == 0, core == CORES - 1
    if own:
        copies = [
            pltpu.make_async_copy(taps_hbm, taps_ref, sems.at[0]),
            pltpu.make_async_copy(weights_hbm, weights_ref, sems.at[1]),
            pltpu.make_async_copy(echoes_hbm, echoes_ref, sems.at[2]),
        ]
        for copy in copies:
            copy.start()
        copies[0].wait()
        copies[1].wait()
        real = toeplitz(taps_ref[0:1, :], BLOCK, sections * BLOCK)
        imag = toeplitz(taps_ref[1:2, :], BLOCK, sections * BLOCK)
        for kind, values in enumerate((real, imag, real - imag)):
            table[kind, 0], table[kind, 1] = split(values)
        settings[...] = settings_of(lines, shift_ref, weights_ref)
        copies[2].wait()

    def piece(segment, part, block):
        at = (CORES * segment + core) * width + block - halo - 1
        low = segment == 0 and block <= halo
        high = segment == segments - 1 and block > halo + width
        if low:
            at = jnp.maximum(at, 0)
        if high:
            at = jnp.minimum(at, blocks - 1)
        values = echoes_ref[part, :, pl.ds(pl.multiple_of(at * BLOCK, BLOCK), BLOCK)]
        if low:
            values = jnp.where(at_start, 0.0, values)
        if high:
            values = jnp.where(at_end, 0.0, values)
        return values

    for segment in range(segments):
        for offset, ref in ((0, even), (1, odd)):
            for pair in range((span - offset) // 2):
                first = 2 * pair + offset
                parts = [
                    jnp.concatenate([piece(segment, part, first), piece(segment, part, first + 1)], axis=0)
                    for part in range(2)
                ]
                at = slice((segment * span + 2 * pair) * lines, (segment * span + 2 * pair + 2) * lines)
                for kind, values in enumerate((parts[0], parts[1], parts[0] + parts[1])):
                    ref[kind, 0, at, :], ref[kind, 1, at, :] = split(values)
    rows = (width + 2) * lines
    products = []
    for kind in range(3):
        sums = None
        for section in range(sections):
            ref = even if section % 2 == 0 else odd
            starts = [(segment * span + section - section % 2) * lines for segment in range(segments)]
            x_high, x_low = [
                jnp.concatenate([ref[kind, which, start : start + rows, :] for start in starts], axis=0)
                for which in range(2)
            ]
            at = slice(section * BLOCK, (section + 1) * BLOCK)
            t_high, t_low = table[kind, 0, :, at], table[kind, 1, :, at]
            for left, right in ((x_high, t_high), (x_low, t_high), (x_high, t_low)):
                term = lax.dot_general(left, right, ROWS_BY_ROWS, preferred_element_type=jnp.float32)
                sums = term if sums is None else sums + term
        products.append(sums)
    compressed[0] = products[0] + products[1]
    compressed[1] = products[2] - products[0] + products[1]
    for part in range(2):
        low, high = slice(0, lines), slice(segments * rows - lines, segments * rows)
        compressed[part, low, :] = jnp.where(at_start, 0.0, compressed[part, low, :])
        compressed[part, high, :] = jnp.where(at_end, 0.0, compressed[part, high, :])

    plan = migration_plan(settings[...])
    sends = []
    run = width // levels
    for step in range(levels):
        level = (lax.axis_index("gy") // inner) ^ DISTANCES[step] if own else step
        streams = [(segment, part) for segment in range(segments) for part in range(2)]

        def loader(segment, part):
            first = (segment * (width + 2) + 1 + level * run) * lines

            def load(tile):
                block, at = tile * LANE // BLOCK, tile * LANE % BLOCK
                start = first + block * lines
                if own:
                    start = pl.multiple_of(start, lines)
                return compressed[part, pl.ds(start, lines), at : at + LANE]

            return load

        moved = migrate(run * BLOCK // LANE, plan, [loader(*stream) for stream in streams])
        for (segment, part), row in zip(streams, moved):
            target = (outs[step] if own else ready.at[step]).at[segment]
            per = target.shape[-1] // LANE
            for tile, values in enumerate(row):
                at = (tile % per) * LANE
                target[tile // per, part * lines : (part + 1) * lines, at : at + LANE] = values
        if not own:
            for segment in range(segments):
                first = (segment * levels + step) * inner
                sends.append(
                    pltpu.make_async_copy(
                        ready.at[step, segment], out_ref.at[first : first + inner], sems.at[step, segment]
                    )
                )
                sends[-1].start()
    for send in sends:
        send.wait()


def settings_of(lines, shift_ref, weights_ref):
    lane = lax.broadcasted_iota(jnp.int32, (lines, LANE), 1)
    row = lax.broadcasted_iota(jnp.int32, (lines, LANE), 0)
    settings = jnp.zeros((lines, LANE), jnp.float32)
    for line in range(lines):
        settings = jnp.where((row == line) & (lane == TAPS), shift_ref[line].astype(jnp.float32), settings)
    for j in range(TAPS):
        settings = jnp.where(lane == j, weights_ref[:, j : j + 1], settings)
    return settings


def migration_plan(settings):
    lines = settings.shape[0]
    lane = lax.broadcasted_iota(jnp.int32, (lines, LANE), 1)
    columns = [jnp.broadcast_to(settings[:, j : j + 1], (lines, LANE)) for j in range(TAPS + 1)]
    shift = columns[TAPS].astype(jnp.int32)
    steps = []
    for step in range(2):
        place = lane + shift - (TAPS // 2 - 1) + step
        steps.append((place & (LANE - 1), place < 0, place >= LANE))
    return steps, columns[:TAPS], lane


def migrate(tiles, plan, loads):
    steps, weights, lane = plan
    pairs = []
    for index, below, above in steps:
        turned = [
            [
                jnp.take_along_axis(load(tile), index, axis=1, mode="promise_in_bounds")
                for tile in range(-1, tiles + 2)
            ]
            for load in loads
        ]
        pairs.append(
            [
                [
                    jnp.where(below, row[tile], jnp.where(above, row[tile + 2], row[tile + 1]))
                    for tile in range(tiles + 1)
                ]
                for row in turned
            ]
        )
    totals = None
    for k in range(TAPS // 2):
        terms = [
            [weights[2 * k] * one + weights[2 * k + 1] * two for one, two in zip(*rows)] for rows in zip(*pairs)
        ]
        if k == 0:
            totals = [row[:tiles] for row in terms]
            continue
        rolled = [[pltpu.roll(term, LANE - 2 * k, axis=1) for term in row] for row in terms]
        inside = lane < LANE - 2 * k
        totals = [
            [total[tile] + jnp.where(inside, row[tile], row[tile + 1]) for tile in range(tiles)]
            for total, row in zip(totals, rolled)
        ]
    return totals


def range_call(own, planes, echoes, taps, *settings):
    lines, range_total = echoes.shape[1], echoes.shape[2]
    blocks = range_total // BLOCK
    sections = (taps.shape[1] if own else taps.shape[-1] - BLOCK) // BLOCK + 1
    segments, levels, inner = planes
    bins = range_total // (CORES * segments * levels * inner)
    width = blocks // (CORES * segments)
    span = width + sections + 1
    flops = 2 * 3 * 3 * segments * (width + 2) * lines * sections * BLOCK * BLOCK
    vmem, hbm = pl.BlockSpec(memory_space=pltpu.VMEM), pl.BlockSpec(memory_space=pltpu.HBM)
    scratch = [
        pltpu.VMEM((3, 2, segments * span * lines, BLOCK), jnp.bfloat16),
        pltpu.VMEM((3, 2, segments * span * lines, BLOCK), jnp.bfloat16),
        pltpu.VMEM((2, segments * (width + 2) * lines, BLOCK), jnp.float32),
    ]
    if own:
        shift_bins, weights = settings
        operands = [shift_bins, taps, weights, echoes]
        operands = [pltpu.with_memory_space_constraint(array, pltpu.HBM) for array in operands]
        in_specs = [pl.BlockSpec(memory_space=pltpu.SMEM), hbm, hbm, hbm]
        out_shape = [jax.ShapeDtypeStruct((segments, inner, 2 * lines, bins), jnp.float32)] * levels
        out_shape += [jax.ShapeDtypeStruct((lines, LANE), jnp.float32)]
        out_shape += [jax.ShapeDtypeStruct((3, 2, BLOCK, sections * BLOCK), jnp.bfloat16)]
        out_specs = [vmem] * (levels + 2)
        scratch = [
            pltpu.VMEM(taps.shape, jnp.float32),
            pltpu.VMEM(weights.shape, jnp.float32),
            pltpu.VMEM(echoes.shape, jnp.float32),
            *scratch,
            pltpu.SemaphoreType.DMA((3,)),
        ]
    else:
        operands = [*settings, taps, echoes]
        in_specs = [vmem] * 3
        out_shape = jax.ShapeDtypeStruct((segments * levels * inner, 2 * lines, bins), jnp.float32)
        out_specs = hbm
        scratch += [
            pltpu.VMEM((levels, segments, inner, 2 * lines, bins), jnp.float32),
            pltpu.SemaphoreType.DMA((levels, segments)),
        ]
    return pl.pallas_call(
        functools.partial(range_kernel, own, planes, lines, blocks, sections),
        out_shape=out_shape,
        in_specs=in_specs,
        out_specs=out_specs,
        scratch_shapes=scratch,
        compiler_params=pltpu.CompilerParams(vmem_limit_bytes=24 << 20),
        cost_estimate=pl.CostEstimate(flops=flops, bytes_accessed=3 * echoes.size * 2, transcendentals=0),
        name="range_own" if own else "range_partner",
    )(*operands)


def regroup_kernel(levels, plane, *refs):
    sources, outs = refs[:levels], refs[levels:]
    inner = sources[0].shape[1]
    mine = place_here(inner)
    for q in range(plane):
        place = mine ^ q
        for k in range(levels):
            outs[q][k] = sources[k][place // inner, lax.rem(place, inner)]


def place_here(inner):
    return (lax.axis_index("gx") // CORES) * inner + lax.rem(lax.axis_index("gy"), inner)


def regroup_call(received):
    levels = len(received)
    segments, inner, rows, bins = received[0].shape
    plane = segments * inner
    return pl.pallas_call(
        functools.partial(regroup_kernel, levels, plane),
        out_shape=[jax.ShapeDtypeStruct((levels, rows, bins), jnp.float32)] * plane,
        in_specs=[pl.BlockSpec(memory_space=pltpu.VMEM)] * levels,
        out_specs=[pl.BlockSpec(memory_space=pltpu.VMEM)] * plane,
        compiler_params=pltpu.CompilerParams(vmem_limit_bytes=8 << 20),
        cost_estimate=pl.CostEstimate(flops=0, bytes_accessed=8 * levels * plane * rows * bins, transcendentals=0),
        name="regroup",
    )(*received)


def azimuth_tables(taps_ref, table):
    length = taps_ref.shape[1]
    diagonals = table.shape[2]
    first = (length // BLOCK + 1 - diagonals) // 2
    zeros = jnp.zeros((1, BLOCK), jnp.float32)
    width = (diagonals + 1) * BLOCK
    full = []
    for part in range(2):
        row = jnp.concatenate([zeros, taps_ref[part : part + 1, :], zeros], axis=1)
        full.append(toeplitz(row[:, first * BLOCK : first * BLOCK + width], BLOCK, width))
    for kind, values in enumerate((full[0], full[1], full[0] - full[1])):
        for n in range(diagonals):
            at = (n + 1) * BLOCK
            table[kind, 0, n], table[kind, 1, n] = split(values[:, at : at + BLOCK])


def azimuth_sums(table, lines_ref):
    diagonals = table.shape[2]
    middle = diagonals // 2
    blocks = lines_ref.shape[1] // BLOCK
    pieces = [[], [], []]
    for b in range(blocks):
        real, imag = [lines_ref[part, b * BLOCK : (b + 1) * BLOCK, :] for part in range(2)]
        for kind, values in enumerate((real, imag, real + imag)):
            pieces[kind].append(split(values))

    def product(b, kind):
        sums = None
        for diagonal in range(diagonals):
            other = b + diagonal - middle
            if not 0 <= other < blocks:
                continue
            m_high, m_low = pieces[kind][other]
            t_high, t_low = table[kind, 0, diagonal], table[kind, 1, diagonal]
            for left, right in ((t_high, m_high), (t_high, m_low), (t_low, m_high)):
                term = lax.dot_general(left, right, PLAIN, preferred_element_type=jnp.float32)
                sums = term if sums is None else sums + term
        return sums

    for b in range(blocks):
        at = slice(b * BLOCK, (b + 1) * BLOCK)
        first, second = product(b, 0), product(b, 1)
        yield 0, at, first + second
        yield 1, at, product(b, 2) - first + second


def azimuth_kernel(planes, *refs):
    segments, levels, inner = planes
    table, moved_ref, *arrived, out_hbm, lines_ref, image, sems = refs
    lines = moved_ref.shape[1] // 2
    run = levels * inner
    core = lax.rem(lax.axis_index("gx"), CORES)
    level = lax.axis_index("gy") // inner
    mine = place_here(inner)
    for q, source in enumerate(arrived):
        place = mine ^ q
        for k in range(levels):
            device = (((place // inner) * CORES + core) * levels + (level ^ DISTANCES[k])) * inner + lax.rem(place, inner)
            rows = pl.ds(pl.multiple_of(device * lines, lines), lines)
            for part in range(2):
                lines_ref[part, rows, :] = source[k, part * lines : (part + 1) * lines, :]
    for segment in range(segments):
        first = (CORES * segment + 1 - core) * run * lines
        rows = pl.ds(pl.multiple_of(first, run * lines), run * lines)
        for part in range(2):
            values = moved_ref[segment * run : (segment + 1) * run, part * lines : (part + 1) * lines, :]
            lines_ref[part, rows, :] = values.reshape(run * lines, values.shape[-1])
    sends = []
    for part, at, sums in azimuth_sums(table, lines_ref):
        image[part, at, :] = sums
        sends.append(pltpu.make_async_copy(image.at[part, at], out_hbm.at[part, at], sems.at[len(sends)]))
        sends[-1].start()
    for send in sends:
        send.wait()


def azimuth_call(planes, count, table, moved, arrived):
    bins = moved.shape[-1]
    vmem = pl.BlockSpec(memory_space=pltpu.VMEM)
    return pl.pallas_call(
        functools.partial(azimuth_kernel, planes),
        out_shape=jax.ShapeDtypeStruct((2, count, bins), jnp.float32),
        in_specs=[vmem] * (2 + len(arrived)),
        out_specs=pl.BlockSpec(memory_space=pltpu.HBM),
        scratch_shapes=[
            pltpu.VMEM((2, count, bins), jnp.float32),
            pltpu.VMEM((2, count, bins), jnp.float32),
            pltpu.SemaphoreType.DMA((2 * count // BLOCK,)),
        ],
        compiler_params=pltpu.CompilerParams(vmem_limit_bytes=24 << 20),
        cost_estimate=pl.CostEstimate(
            flops=2 * 3 * 4 * count * BLOCK * bins, bytes_accessed=4 * 4 * count * bins, transcendentals=0
        ),
        name="azimuth",
    )(table, moved, *arrived)


def table_call(azimuth_ref, count):
    diagonals = min(azimuth_ref.shape[1] // BLOCK + 1, 2 * (count // BLOCK) - 1)
    vmem = pl.BlockSpec(memory_space=pltpu.VMEM)
    return pl.pallas_call(
        azimuth_tables,
        out_shape=jax.ShapeDtypeStruct((3, 2, diagonals, BLOCK, BLOCK), jnp.bfloat16),
        in_specs=[vmem],
        out_specs=vmem,
        compiler_params=pltpu.CompilerParams(vmem_limit_bytes=24 << 20),
        cost_estimate=pl.CostEstimate(flops=AHEAD << 20, bytes_accessed=0, transcendentals=0),
        name="azimuth_table",
    )(azimuth_ref)


def pairs_of(planes, level_step=0, place_step=0, core_step=0):
    segments, levels, inner = planes
    pairs = []
    for device in range(CORES * segments * levels * inner):
        core = (device // (levels * inner)) % CORES
        place = (device // (CORES * levels * inner)) * inner + device % inner
        level = (device // inner) % levels
        place, level, core = place ^ place_step, level ^ level_step, core ^ core_step
        pairs.append((device, (((place // inner) * CORES + core) * levels + level) * inner + place % inner))
    return pairs


def per_device(echoes, range_ref, azimuth_ref, shift_bins, interp_weights):
    outer, run = lax.axis_size("gx"), lax.axis_size("gy")
    segments, levels = outer // CORES, len(DISTANCES)
    planes = (segments, levels, run // levels)
    devices_all = outer * run
    bins = echoes.shape[2] // devices_all
    *by_level, settings, table = range_call(True, planes, echoes, range_ref, shift_bins, interp_weights)
    received = [by_level[0]] + [
        lax.ppermute(array, AXES, pairs_of(planes, level_step=distance))
        for distance, array in zip(DISTANCES[1:], by_level[1:])
    ]
    settings, echoes_later = lax.optimization_barrier((settings, echoes))
    echoes_partner = lax.ppermute(echoes_later, AXES, pairs_of(planes, core_step=1))
    settings_partner = lax.ppermute(settings, AXES, pairs_of(planes, core_step=1))
    migrated = range_call(False, planes, echoes_partner, table, settings_partner)
    groups = [
        [(segment * CORES + core) * run + at for segment in range(segments) for at in range(run)]
        for core in range(CORES)
    ]
    moved = lax.all_to_all(migrated, AXES, split_axis=0, concat_axis=0, axis_index_groups=groups, tiled=True)
    *received, migrated = lax.optimization_barrier((*received, migrated))
    by_place = regroup_call(received)
    *by_place, taps_later = lax.optimization_barrier((*by_place, azimuth_ref))
    arrived = [by_place[0]] + [
        lax.ppermute(by_place[q], AXES, pairs_of(planes, place_step=q)) for q in range(1, len(by_place))
    ]
    count = devices_all * echoes.shape[1]
    return azimuth_call(planes, count, table_call(taps_later, count), moved, arrived)


def solution(mesh):
    placed = (P(None, AXES, None), P(), P(), P(AXES), P(AXES, None))
    return jax.shard_map(
        per_device,
        mesh=mesh,
        in_specs=placed,
        out_specs=P(None, None, AXES),
        check_vma=False,
    )
```

```python
import functools

import jax
import jax.numpy as jnp
from jax import lax
from jax.experimental import pallas as pl
from jax.experimental.pallas import tpu as pltpu
from jax.sharding import PartitionSpec as P

TAPS = 8
BLOCK = 256
LANE = 128
AXES = ("gx", "gy")
CORES = 2
DISTANCES = (0, 2, 3, 1)
AHEAD = 20000

ROWS_BY_ROWS = (((1,), (1,)), ((), ()))
PLAIN = (((1,), (0,)), ((), ()))


def split(values):
    high = values.astype(jnp.bfloat16)
    return high, (values - high.astype(jnp.float32)).astype(jnp.bfloat16)


def toeplitz(row, rows, width):
    if width > row.shape[1]:
        row = jnp.concatenate([row, jnp.zeros((1, width - row.shape[1]), jnp.float32)], axis=1)
    return pltpu.roll(jnp.broadcast_to(row, (rows, width)), 0, axis=1, stride=1, stride_axis=0)


def range_kernel(own, planes, lines, blocks, sections, *refs):
    if own:
        shift_ref, taps_hbm, weights_hbm, echoes_hbm, *outs, settings, table, taps_ref, weights_ref, echoes_ref, even, odd, compressed, sems = refs
    else:
        settings, table, echoes_ref, out_ref, even, odd, compressed, ready, sems = refs
    segments, levels, inner = planes
    core = lax.rem(lax.axis_index("gx"), CORES)
    width = blocks // (CORES * segments)
    halo = (sections - 1) // 2
    span = width + 2 + 2 * halo
    at_start, at_end = core == 0, core == CORES - 1
    if own:
        copies = [
            pltpu.make_async_copy(taps_hbm, taps_ref, sems.at[0]),
            pltpu.make_async_copy(weights_hbm, weights_ref, sems.at[1]),
            pltpu.make_async_copy(echoes_hbm, echoes_ref, sems.at[2]),
        ]
        for copy in copies:
            copy.start()
        copies[0].wait()
        copies[1].wait()
        real = toeplitz(taps_ref[0:1, :], BLOCK, sections * BLOCK)
        imag = toeplitz(taps_ref[1:2, :], BLOCK, sections * BLOCK)
        for kind, values in enumerate((real, imag, real - imag)):
            table[kind, 0], table[kind, 1] = split(values)
        settings[...] = settings_of(lines, shift_ref, weights_ref)
        copies[2].wait()

    def piece(segment, part, block):
        at = (CORES * segment + core) * width + block - halo - 1
        low = segment == 0 and block <= halo
        high = segment == segments - 1 and block > halo + width
        if low:
            at = jnp.maximum(at, 0)
        if high:
            at = jnp.minimum(at, blocks - 1)
        values = echoes_ref[part, :, pl.ds(pl.multiple_of(at * BLOCK, BLOCK), BLOCK)]
        if low:
            values = jnp.where(at_start, 0.0, values)
        if high:
            values = jnp.where(at_end, 0.0, values)
        return values

    for segment in range(segments):
        for offset, ref in ((0, even), (1, odd)):
            for pair in range((span - offset) // 2):
                first = 2 * pair + offset
                parts = [
                    jnp.concatenate([piece(segment, part, first), piece(segment, part, first + 1)], axis=0)
                    for part in range(2)
                ]
                at = slice((segment * span + 2 * pair) * lines, (segment * span + 2 * pair + 2) * lines)
                for kind, values in enumerate((parts[0], parts[1], parts[0] + parts[1])):
                    ref[kind, 0, at, :], ref[kind, 1, at, :] = split(values)
    rows = (width + 2) * lines
    products = []
    for kind in range(3):
        sums = None
        for section in range(sections):
            ref = even if section % 2 == 0 else odd
            starts = [(segment * span + section - section % 2) * lines for segment in range(segments)]
            x_high, x_low = [
                jnp.concatenate([ref[kind, which, start : start + rows, :] for start in starts], axis=0)
                for which in range(2)
            ]
            at = slice(section * BLOCK, (section + 1) * BLOCK)
            t_high, t_low = table[kind, 0, :, at], table[kind, 1, :, at]
            for left, right in ((x_high, t_high), (x_low, t_high), (x_high, t_low)):
                term = lax.dot_general(left, right, ROWS_BY_ROWS, preferred_element_type=jnp.float32)
                sums = term if sums is None else sums + term
        products.append(sums)
    compressed[0] = products[0] + products[1]
    compressed[1] = products[2] - products[0] + products[1]
    for part in range(2):
        low, high = slice(0, lines), slice(segments * rows - lines, segments * rows)
        compressed[part, low, :] = jnp.where(at_start, 0.0, compressed[part, low, :])
        compressed[part, high, :] = jnp.where(at_end, 0.0, compressed[part, high, :])

    plan = migration_plan(settings[...])
    sends = []
    run = width // levels
    for step in range(levels):
        level = (lax.axis_index("gy") // inner) ^ DISTANCES[step] if own else step
        streams = [(segment, part) for segment in range(segments) for part in range(2)]

        def loader(segment, part):
            first = (segment * (width + 2) + 1 + level * run) * lines

            def load(tile):
                block, at = tile * LANE // BLOCK, tile * LANE % BLOCK
                start = first + block * lines
                if own:
                    start = pl.multiple_of(start, lines)
                return compressed[part, pl.ds(start, lines), at : at + LANE]

            return load

        moved = migrate(run * BLOCK // LANE, plan, [loader(*stream) for stream in streams])
        for (segment, part), row in zip(streams, moved):
            target = (outs[step] if own else ready.at[step]).at[segment]
            per = target.shape[-1] // LANE
            for tile, values in enumerate(row):
                at = (tile % per) * LANE
                target[tile // per, part * lines : (part + 1) * lines, at : at + LANE] = values
        if not own:
            for segment in range(segments):
                first = (segment * levels + step) * inner
                sends.append(
                    pltpu.make_async_copy(
                        ready.at[step, segment], out_ref.at[first : first + inner], sems.at[step, segment]
                    )
                )
                sends[-1].start()
    for send in sends:
        send.wait()


def settings_of(lines, shift_ref, weights_ref):
    lane = lax.broadcasted_iota(jnp.int32, (lines, LANE), 1)
    row = lax.broadcasted_iota(jnp.int32, (lines, LANE), 0)
    settings = jnp.zeros((lines, LANE), jnp.float32)
    for line in range(lines):
        settings = jnp.where((row == line) & (lane == TAPS), shift_ref[line].astype(jnp.float32), settings)
    for j in range(TAPS):
        settings = jnp.where(lane == j, weights_ref[:, j : j + 1], settings)
    return settings


def migration_plan(settings):
    lines = settings.shape[0]
    lane = lax.broadcasted_iota(jnp.int32, (lines, LANE), 1)
    columns = [jnp.broadcast_to(settings[:, j : j + 1], (lines, LANE)) for j in range(TAPS + 1)]
    shift = columns[TAPS].astype(jnp.int32)
    steps = []
    for step in range(2):
        place = lane + shift - (TAPS // 2 - 1) + step
        steps.append((place & (LANE - 1), place < 0, place >= LANE))
    return steps, columns[:TAPS], lane


def migrate(tiles, plan, loads):
    steps, weights, lane = plan
    pairs = []
    for index, below, above in steps:
        turned = [
            [
                jnp.take_along_axis(load(tile), index, axis=1, mode="promise_in_bounds")
                for tile in range(-1, tiles + 2)
            ]
            for load in loads
        ]
        pairs.append(
            [
                [
                    jnp.where(below, row[tile], jnp.where(above, row[tile + 2], row[tile + 1]))
                    for tile in range(tiles + 1)
                ]
                for row in turned
            ]
        )
    totals = None
    for k in range(TAPS // 2):
        terms = [
            [weights[2 * k] * one + weights[2 * k + 1] * two for one, two in zip(*rows)] for rows in zip(*pairs)
        ]
        if k == 0:
            totals = [row[:tiles] for row in terms]
            continue
        rolled = [[pltpu.roll(term, LANE - 2 * k, axis=1) for term in row] for row in terms]
        inside = lane < LANE - 2 * k
        totals = [
            [total[tile] + jnp.where(inside, row[tile], row[tile + 1]) for tile in range(tiles)]
            for total, row in zip(totals, rolled)
        ]
    return totals


def range_call(own, planes, echoes, taps, *settings):
    lines, range_total = echoes.shape[1], echoes.shape[2]
    blocks = range_total // BLOCK
    sections = (taps.shape[1] if own else taps.shape[-1] - BLOCK) // BLOCK + 1
    segments, levels, inner = planes
    bins = range_total // (CORES * segments * levels * inner)
    width = blocks // (CORES * segments)
    span = width + sections + 1
    flops = 2 * 3 * 3 * segments * (width + 2) * lines * sections * BLOCK * BLOCK
    vmem, hbm = pl.BlockSpec(memory_space=pltpu.VMEM), pl.BlockSpec(memory_space=pltpu.HBM)
    scratch = [
        pltpu.VMEM((3, 2, segments * span * lines, BLOCK), jnp.bfloat16),
        pltpu.VMEM((3, 2, segments * span * lines, BLOCK), jnp.bfloat16),
        pltpu.VMEM((2, segments * (width + 2) * lines, BLOCK), jnp.float32),
    ]
    if own:
        shift_bins, weights = settings
        operands = [shift_bins, taps, weights, echoes]
        operands = [pltpu.with_memory_space_constraint(array, pltpu.HBM) for array in operands]
        in_specs = [pl.BlockSpec(memory_space=pltpu.SMEM), hbm, hbm, hbm]
        out_shape = [jax.ShapeDtypeStruct((segments, inner, 2 * lines, bins), jnp.float32)] * levels
        out_shape += [jax.ShapeDtypeStruct((lines, LANE), jnp.float32)]
        out_shape += [jax.ShapeDtypeStruct((3, 2, BLOCK, sections * BLOCK), jnp.bfloat16)]
        out_specs = [vmem] * (levels + 2)
        scratch = [
            pltpu.VMEM(taps.shape, jnp.float32),
            pltpu.VMEM(weights.shape, jnp.float32),
            pltpu.VMEM(echoes.shape, jnp.float32),
            *scratch,
            pltpu.SemaphoreType.DMA((3,)),
        ]
    else:
        operands = [*settings, taps, echoes]
        in_specs = [vmem] * 3
        out_shape = jax.ShapeDtypeStruct((segments * levels * inner, 2 * lines, bins), jnp.float32)
        out_specs = hbm
        scratch += [
            pltpu.VMEM((levels, segments, inner, 2 * lines, bins), jnp.float32),
            pltpu.SemaphoreType.DMA((levels, segments)),
        ]
    return pl.pallas_call(
        functools.partial(range_kernel, own, planes, lines, blocks, sections),
        out_shape=out_shape,
        in_specs=in_specs,
        out_specs=out_specs,
        scratch_shapes=scratch,
        compiler_params=pltpu.CompilerParams(vmem_limit_bytes=24 << 20),
        cost_estimate=pl.CostEstimate(flops=flops, bytes_accessed=3 * echoes.size * 2, transcendentals=0),
        name="range_own" if own else "range_partner",
    )(*operands)


def regroup_kernel(levels, plane, *refs):
    sources, outs = refs[:levels], refs[levels:]
    inner = sources[0].shape[1]
    mine = place_here(inner)
    for q in range(plane):
        place = mine ^ q
        for k in range(levels):
            outs[q][k] = sources[k][place // inner, lax.rem(place, inner)]


def place_here(inner):
    return (lax.axis_index("gx") // CORES) * inner + lax.rem(lax.axis_index("gy"), inner)


def regroup_call(received):
    levels = len(received)
    segments, inner, rows, bins = received[0].shape
    plane = segments * inner
    return pl.pallas_call(
        functools.partial(regroup_kernel, levels, plane),
        out_shape=[jax.ShapeDtypeStruct((levels, rows, bins), jnp.float32)] * plane,
        in_specs=[pl.BlockSpec(memory_space=pltpu.VMEM)] * levels,
        out_specs=[pl.BlockSpec(memory_space=pltpu.VMEM)] * plane,
        compiler_params=pltpu.CompilerParams(vmem_limit_bytes=8 << 20),
        cost_estimate=pl.CostEstimate(flops=0, bytes_accessed=8 * levels * plane * rows * bins, transcendentals=0),
        name="regroup",
    )(*received)


def azimuth_tables(taps_ref, table):
    length = taps_ref.shape[1]
    diagonals = table.shape[2]
    first = (length // BLOCK + 1 - diagonals) // 2
    zeros = jnp.zeros((1, BLOCK), jnp.float32)
    for part in range(2):
        row = jnp.concatenate([zeros, taps_ref[part : part + 1, :], zeros], axis=1)
        width = (diagonals + 1) * BLOCK
        full = toeplitz(row[:, first * BLOCK : first * BLOCK + width], BLOCK, width)
        for n in range(diagonals):
            at = (n + 1) * BLOCK
            table[part, 0, n], table[part, 1, n] = split(full[:, at : at + BLOCK])


def azimuth_sums(table, lines_ref):
    diagonals = table.shape[2]
    middle = diagonals // 2
    blocks = lines_ref.shape[1] // BLOCK
    pieces = [
        [split(lines_ref[part, b * BLOCK : (b + 1) * BLOCK, :]) for b in range(blocks)] for part in range(2)
    ]

    def product(b, taps, part):
        sums = None
        for diagonal in range(diagonals):
            other = b + diagonal - middle
            if not 0 <= other < blocks:
                continue
            m_high, m_low = pieces[part][other]
            t_high, t_low = table[taps, 0, diagonal], table[taps, 1, diagonal]
            for left, right in ((t_high, m_high), (t_high, m_low), (t_low, m_high)):
                term = lax.dot_general(left, right, PLAIN, preferred_element_type=jnp.float32)
                sums = term if sums is None else sums + term
        return sums

    for b in range(blocks):
        at = slice(b * BLOCK, (b + 1) * BLOCK)
        yield 0, at, product(b, 0, 0) + product(b, 1, 1)
        yield 1, at, product(b, 0, 1) - product(b, 1, 0)


def azimuth_kernel(planes, *refs):
    segments, levels, inner = planes
    table, moved_ref, *arrived, out_hbm, lines_ref, image, sems = refs
    lines = moved_ref.shape[1] // 2
    run = levels * inner
    core = lax.rem(lax.axis_index("gx"), CORES)
    level = lax.axis_index("gy") // inner
    mine = place_here(inner)
    for q, source in enumerate(arrived):
        place = mine ^ q
        for k in range(levels):
            device = (((place // inner) * CORES + core) * levels + (level ^ DISTANCES[k])) * inner + lax.rem(place, inner)
            rows = pl.ds(pl.multiple_of(device * lines, lines), lines)
            for part in range(2):
                lines_ref[part, rows, :] = source[k, part * lines : (part + 1) * lines, :]
    for segment in range(segments):
        first = (CORES * segment + 1 - core) * run * lines
        rows = pl.ds(pl.multiple_of(first, run * lines), run * lines)
        for part in range(2):
            values = moved_ref[segment * run : (segment + 1) * run, part * lines : (part + 1) * lines, :]
            lines_ref[part, rows, :] = values.reshape(run * lines, values.shape[-1])
    sends = []
    for part, at, sums in azimuth_sums(table, lines_ref):
        image[part, at, :] = sums
        sends.append(pltpu.make_async_copy(image.at[part, at], out_hbm.at[part, at], sems.at[len(sends)]))
        sends[-1].start()
    for send in sends:
        send.wait()


def azimuth_call(planes, count, table, moved, arrived):
    bins = moved.shape[-1]
    vmem = pl.BlockSpec(memory_space=pltpu.VMEM)
    return pl.pallas_call(
        functools.partial(azimuth_kernel, planes),
        out_shape=jax.ShapeDtypeStruct((2, count, bins), jnp.float32),
        in_specs=[vmem] * (2 + len(arrived)),
        out_specs=pl.BlockSpec(memory_space=pltpu.HBM),
        scratch_shapes=[
            pltpu.VMEM((2, count, bins), jnp.float32),
            pltpu.VMEM((2, count, bins), jnp.float32),
            pltpu.SemaphoreType.DMA((2 * count // BLOCK,)),
        ],
        compiler_params=pltpu.CompilerParams(vmem_limit_bytes=24 << 20),
        cost_estimate=pl.CostEstimate(
            flops=2 * 3 * 4 * count * BLOCK * bins, bytes_accessed=4 * 4 * count * bins, transcendentals=0
        ),
        name="azimuth",
    )(table, moved, *arrived)


def table_call(azimuth_ref, count):
    diagonals = min(azimuth_ref.shape[1] // BLOCK + 1, 2 * (count // BLOCK) - 1)
    vmem = pl.BlockSpec(memory_space=pltpu.VMEM)
    return pl.pallas_call(
        azimuth_tables,
        out_shape=jax.ShapeDtypeStruct((2, 2, diagonals, BLOCK, BLOCK), jnp.bfloat16),
        in_specs=[vmem],
        out_specs=vmem,
        compiler_params=pltpu.CompilerParams(vmem_limit_bytes=24 << 20),
        cost_estimate=pl.CostEstimate(flops=AHEAD << 20, bytes_accessed=0, transcendentals=0),
        name="azimuth_table",
    )(azimuth_ref)


def pairs_of(planes, level_step=0, place_step=0, core_step=0):
    segments, levels, inner = planes
    pairs = []
    for device in range(CORES * segments * levels * inner):
        core = (device // (levels * inner)) % CORES
        place = (device // (CORES * levels * inner)) * inner + device % inner
        level = (device // inner) % levels
        place, level, core = place ^ place_step, level ^ level_step, core ^ core_step
        pairs.append((device, (((place // inner) * CORES + core) * levels + level) * inner + place % inner))
    return pairs


def per_device(echoes, range_ref, azimuth_ref, shift_bins, interp_weights):
    outer, run = lax.axis_size("gx"), lax.axis_size("gy")
    segments, levels = outer // CORES, len(DISTANCES)
    planes = (segments, levels, run // levels)
    devices_all = outer * run
    bins = echoes.shape[2] // devices_all
    echoes_partner = lax.ppermute(echoes, AXES, pairs_of(planes, core_step=1))
    *by_level, settings, table = range_call(True, planes, echoes, range_ref, shift_bins, interp_weights)
    received = [by_level[0]] + [
        lax.ppermute(array, AXES, pairs_of(planes, level_step=distance))
        for distance, array in zip(DISTANCES[1:], by_level[1:])
    ]
    settings_partner = lax.ppermute(settings, AXES, pairs_of(planes, core_step=1))
    migrated = range_call(False, planes, echoes_partner, table, settings_partner)
    groups = [
        [(segment * CORES + core) * run + at for segment in range(segments) for at in range(run)]
        for core in range(CORES)
    ]
    moved = lax.all_to_all(migrated, AXES, split_axis=0, concat_axis=0, axis_index_groups=groups, tiled=True)
    *received, migrated = lax.optimization_barrier((*received, migrated))
    by_place = regroup_call(received)
    *by_place, taps_later = lax.optimization_barrier((*by_place, azimuth_ref))
    arrived = [by_place[0]] + [
        lax.ppermute(by_place[q], AXES, pairs_of(planes, place_step=q)) for q in range(1, len(by_place))
    ]
    count = devices_all * echoes.shape[1]
    return azimuth_call(planes, count, table_call(taps_later, count), moved, arrived)


def solution(mesh):
    placed = (P(None, AXES, None), P(), P(), P(AXES), P(AXES, None))
    return jax.shard_map(
        per_device,
        mesh=mesh,
        in_specs=placed,
        out_specs=P(None, None, AXES),
        check_vma=False,
    )
```
